32 devices in a mesh: region: 8 (over z, y), member: 4 (over x, core).
Axes of the slice: x: 2, y: 2, z: 4, core: 2. Of those that a mesh axis runs over, the one named last changes fastest.
Arguments:
- latent: bfloat16 [4, 2048, 512], P('member', 'region'), may hold values from -6 to 6
- node_gain: float32 [512], replicated, may hold values from 0.1 to 1.9
- w_qkv: bfloat16 [512, 1536], replicated, may hold values from -0.25 to 0.25
- w_out: bfloat16 [512, 512], replicated, may hold values from -0.25 to 0.25
- edge_bias: float32 [2048, 128], P('region'), may hold values from -6 to 400
- edge_source: int32 [2048, 8], P('region'), may hold values from 0 to 511, as said below
- boundary: int32 [8, 256], P('region'), may hold values from 0 to 255, as said below
- node_count: int32 [8], P('region'), may hold values from 128 to 256, as said below
- decoder_projection_weight: bfloat16 [512, 98], replicated, may hold values from -0.25 to 0.25
- dec_source: int32 [3, 8192], P(None, 'region'), may hold values from 0 to 511, as said below
- dec_weight: float32 [3, 8192], P(None, 'region'), may hold values from 0.2 to 1
- state: float32 [98, 8192], P(None, 'region'), may hold values from -6 to 6
- target: float32 [98, 8192], P(None, 'region'), may hold values from -6 to 6
- area: float32 [8192], P('region'), may hold values from 0.3 to 9
- var_weight: float32 [98], replicated, may hold values from 0.3 to 3
Outputs:
- loss: float32 [], replicated
- grad_qkv: float32 [512, 1536], P('region')
- grad_out: float32 [512, 512], P('region')
- decoder_weight_gradient: float32 [512, 98], P('region')
- grad_latent: bfloat16 [4, 2048, 512], P('member', 'region')
The draws below stay inside these ranges and needn't reach their ends.
Inputs may be any that keep to these rules, and one draw needn't show every extreme that they name: Row n of edge_source belongs to region r = n // 256; each entry is below node_count[r], or is 256 + i with i below 256. Row r of boundary holds node slots below node_count[r]. `node_count`: equals 256 in at least one region. `dec_source`: column p belongs to region r = p // 1024; each entry is below node_count[r], or is 256 + i with i below 256.
All inputs are finite; a program needn't handle non-finite values.
Results may differ from the reference program's by a relative error of at most 0.02.
Values may be sent and summed in bfloat16 or wider, within the bound.
No kernel may reach another device: no remote copies, remote signals or barrier semaphores. Data moves between devices by JAX's collectives and lax.ppermute only.
A program may use at most 128 MiB of HBM per device.

```python
import math
import jax
import jax.numpy as jnp
from jax import lax

W = 512
HEADS = 16
K = 8
NDEC = 3
OUTPUT_VARIABLES = 98
NL = 256
BND = 128
REGION_POINTS = 1024
MEMBERS = 4
NODES = 2048
GRID = 8192
N_REGION = 8
N_MEMBER = 4


def region_counts(key):
    region_loss_sum = NODES // NL
    counts = jax.random.randint(jax.random.fold_in(key, 101), (region_loss_sum,), NL // 2, NL + 1)
    fullest = jax.random.randint(jax.random.fold_in(key, 102), (), 0, region_loss_sum)
    return jnp.where(jnp.arange(region_loss_sum) == fullest, NL, counts).astype(jnp.int32)


def local_rows(key, owners, shape, rim_share):
    raw_bits = jax.random.randint(jax.random.fold_in(key, 1), shape, 0, 1 << 24)
    own_rows = raw_bits % owners
    rim_rows = NL + jax.random.randint(jax.random.fold_in(key, 2), shape, 0, 2 * BND)
    chosen = jax.random.randint(jax.random.fold_in(key, 3), shape, 0, rim_share) == 0
    return jnp.where(chosen, rim_rows, own_rows).astype(jnp.int32)


def draw_node_count(key, part):
    return region_counts(key)


def draw_edge_source(key, part):
    counts = region_counts(key)
    owners = counts[jnp.arange(NODES) // NL][:, None]
    return local_rows(jax.random.fold_in(key, 201), owners, (NODES, K), 4)


def draw_boundary(key, part):
    counts = region_counts(key)
    raw_bits = jax.random.randint(jax.random.fold_in(key, 301), (NODES // NL, 2 * BND), 0, 1 << 24)
    return (raw_bits % counts[:, None]).astype(jnp.int32)


def draw_dec_source(key, part):
    counts = region_counts(key)
    owners = counts[jnp.arange(GRID) // REGION_POINTS][None, :]
    return local_rows(jax.random.fold_in(key, 401), owners, (NDEC, GRID), 8)


def draw_edge_bias(key, part):
    base = jnp.clip(jax.random.normal(jax.random.fold_in(key, 501), (NODES, HEADS * K), jnp.float32), -6.0, 6.0)
    return base


def draw_area(key, part):
    ramp = 1.0 + 2.0 * jnp.arange(GRID, dtype=jnp.float32) / GRID
    factor = jnp.exp(jax.random.uniform(jax.random.fold_in(key, 601), (GRID,), jnp.float32, -0.69, 0.69))
    return ramp * factor


def level_of(own_key, shape, cuts, least, largest):
    level = 1.0
    for dim, parts in cuts:
        steps = jax.random.uniform(jax.random.fold_in(jax.random.fold_in(own_key, 6), dim), (parts,), jnp.float32, least / len(cuts), largest / len(cuts))
        level = level * jnp.repeat(jnp.exp(steps), shape[dim] // parts).reshape((-1,) + (1,) * (len(shape) - 1 - dim))
    return level


def noise(key, dims, width, limit, cuts=(), held_as=jnp.bfloat16):
    values = width * jax.random.normal(key, dims, jnp.float32)
    if cuts:
        values = values * level_of(key, dims, cuts, -0.22, 0.18)
    return jnp.clip(values, -limit, limit).astype(held_as)


def setup_inputs(seed: int = 0) -> dict:
    splits = jax.random.split(jax.random.key(seed), 16)
    latent = noise(splits[0], (MEMBERS, NODES, W), 1.0, 6.0, ((0, 4), (1, 8)))
    node_gain = jnp.clip(1.0 + 0.18 * jax.random.normal(splits[1], (W,), jnp.float32), 0.1, 1.9)
    w_qkv = noise(splits[2], (W, 3 * W), W ** -0.5, 0.25)
    w_out = noise(splits[3], (W, W), W ** -0.5, 0.25)
    edge_bias = draw_edge_bias(jax.random.fold_in(splits[15], 71), 0)
    edge_source = draw_edge_source(jax.random.fold_in(splits[15], 71), 0)
    boundary = draw_boundary(jax.random.fold_in(splits[15], 71), 0)
    node_count = draw_node_count(jax.random.fold_in(splits[15], 71), 0)
    decoder_projection_weight = noise(splits[8], (W, OUTPUT_VARIABLES), W ** -0.5, 0.25)
    dec_source = draw_dec_source(jax.random.fold_in(splits[15], 71), 0)
    dec_weight = jnp.clip(jnp.exp(math.log(1.0) - 1.609438 * jax.random.uniform(splits[10], (NDEC, GRID), jnp.float32) ** level_of(splits[10], (NDEC, GRID), ((1, 8),), -0.2, 0.2)), 0.2, 1.0)
    state = noise(splits[11], (OUTPUT_VARIABLES, GRID), 1.0, 6.0, ((1, 8),), jnp.float32)
    target = noise(splits[12], (OUTPUT_VARIABLES, GRID), 1.0, 6.0, ((1, 8),), jnp.float32)
    area = draw_area(jax.random.fold_in(splits[15], 71), 0)
    var_weight = jnp.clip(jnp.exp(jax.random.uniform(splits[14], (OUTPUT_VARIABLES,), jnp.float32, math.log(0.3), math.log(3.0))), 0.3, 3.0)
    return dict(latent=latent, node_gain=node_gain, w_qkv=w_qkv, w_out=w_out, edge_bias=edge_bias, edge_source=edge_source, boundary=boundary, node_count=node_count, decoder_projection_weight=decoder_projection_weight, dec_source=dec_source, dec_weight=dec_weight, state=state, target=target, area=area, var_weight=var_weight)


ALPHA = 0.95
NORM_EPS = 1e-05
SMOOTH_SQ = 0.25
SMOOTH_ROOT = 0.5

def layer_norm(latent_rows, gain):
    values = latent_rows.astype(jnp.float32)
    center = values - lax.optimization_barrier(jnp.mean(values, axis=-1, keepdims=True))
    inverse = lax.rsqrt(lax.optimization_barrier(jnp.mean(center * center, axis=-1, keepdims=True)) + NORM_EPS)
    return (center * inverse * gain).astype(jnp.bfloat16)

def norm_backward(latent_rows, gain, grad_rows):
    values = latent_rows.astype(jnp.float32)
    center = values - lax.optimization_barrier(jnp.mean(values, axis=-1, keepdims=True))
    inverse = lax.rsqrt(lax.optimization_barrier(jnp.mean(center * center, axis=-1, keepdims=True)) + NORM_EPS)
    scaled = center * inverse
    scaled_grad = grad_rows * gain
    return inverse * (scaled_grad - lax.optimization_barrier(jnp.mean(scaled_grad, axis=-1, keepdims=True)) - scaled * lax.optimization_barrier(jnp.mean(scaled_grad * scaled, axis=-1, keepdims=True)))

def attend(queries, key_value, bias_rows, edge_src):
    node_cap, edge_count = edge_src.shape
    feature_width = queries.shape[1]
    head_count = bias_rows.shape[1] // edge_count
    head_size = feature_width // head_count
    picked_rows = key_value[edge_src]
    key_rows = picked_rows[:, :, :feature_width].reshape(node_cap, edge_count, head_count, head_size)
    value_rows = picked_rows[:, :, feature_width:].reshape(node_cap, edge_count, head_count, head_size)
    query_heads = queries.reshape(node_cap, head_count, head_size)
    scores = jnp.einsum('nhd,nehd->nhe', query_heads.astype(jnp.float32), key_rows.astype(jnp.float32)) / math.sqrt(head_size)
    scores = scores + bias_rows.reshape(node_cap, head_count, edge_count)
    shifted = jnp.exp(scores - lax.optimization_barrier(jnp.max(scores, axis=-1, keepdims=True)))
    attn_probs = shifted / lax.optimization_barrier(jnp.sum(shifted, axis=-1, keepdims=True))
    rounded = attn_probs.astype(jnp.bfloat16)
    attended = jnp.einsum('nhe,nehd->nhd', rounded.astype(jnp.float32), value_rows.astype(jnp.float32))
    kept_values = (query_heads, key_rows, value_rows, attn_probs, rounded)
    return (attended.reshape(node_cap, feature_width).astype(jnp.bfloat16), kept_values)

def attend_backward(grad_mixed, kept_values, edge_src, table_rows):
    query_heads, key_rows, value_rows, attn_probs, rounded = kept_values
    node_cap, head_count, head_size = query_heads.shape
    edge_count = edge_src.shape[1]
    feature_width = head_count * head_size
    grad_heads = grad_mixed.reshape(node_cap, head_count, head_size).astype(jnp.float32)
    grad_probs = jnp.einsum('nhd,nehd->nhe', grad_heads, value_rows.astype(jnp.float32))
    grad_scores = (attn_probs * (grad_probs - lax.optimization_barrier(jnp.sum(attn_probs * grad_probs, axis=-1, keepdims=True)))).astype(jnp.bfloat16)
    inv_root = 1.0 / math.sqrt(head_size)
    grad_query = jnp.einsum('nhe,nehd->nhd', grad_scores.astype(jnp.float32), key_rows.astype(jnp.float32)) * inv_root
    grad_query = grad_query.reshape(node_cap, feature_width).astype(jnp.bfloat16)
    grad_keys = jnp.einsum('nhe,nhd->nehd', grad_scores.astype(jnp.float32), query_heads.astype(jnp.float32)) * inv_root
    grad_values = jnp.einsum('nhe,nhd->nehd', rounded.astype(jnp.float32), grad_heads)
    grad_edges = jnp.concatenate([grad_keys.reshape(node_cap * edge_count, feature_width), grad_values.reshape(node_cap * edge_count, feature_width)], axis=1)
    grad_key_value = jax.ops.segment_sum(grad_edges, edge_src.reshape(-1), num_segments=table_rows)
    return (grad_query, grad_key_value.astype(jnp.bfloat16))

def smooth_abs(values):
    return jnp.sqrt(values * values + SMOOTH_SQ) - SMOOTH_ROOT

def smooth_slope(values):
    return values * lax.rsqrt(values * values + SMOOTH_SQ)

def ensemble_score_parts(own_block, every_member_output, target_rows, weight_rows):
    member_score_sum = every_member_output.shape[0]
    fair_scale = 1.0 - (1.0 - ALPHA) / member_score_sum
    pair_scale = fair_scale / (2.0 * member_score_sum * (member_score_sum - 1))
    spread = jnp.zeros_like(own_block)
    slope_sum = jnp.zeros_like(own_block)
    for peer_index in range(member_score_sum):
        member_gap = own_block - every_member_output[peer_index][None]
        spread = spread + smooth_abs(member_gap)
        slope_sum = slope_sum + smooth_slope(member_gap)
    target_gap = own_block - target_rows[None]
    crps_term = smooth_abs(target_gap) / member_score_sum - pair_scale * spread
    grad_rows = (smooth_slope(target_gap) / member_score_sum - 2.0 * pair_scale * slope_sum) * weight_rows[None]
    return (jnp.sum(crps_term * weight_rows[None]), grad_rows.astype(jnp.bfloat16))

def with_rims(own_rows, border_rows):
    rim_size = border_rows.shape[2] // 2
    from_left = jnp.roll(border_rows[:, :, rim_size:], 1, axis=1)
    from_right = jnp.roll(border_rows[:, :, :rim_size], -1, axis=1)
    return jnp.concatenate([own_rows, from_left, from_right], axis=2)

def rims_back(rim_rows):
    rim_size = rim_rows.shape[2] // 2
    to_left = jnp.roll(rim_rows[:, :, rim_size:], 1, axis=1)
    to_right = jnp.roll(rim_rows[:, :, :rim_size], -1, axis=1)
    return jnp.concatenate([to_left, to_right], axis=2)

def reference(latent, node_gain, w_qkv, w_out, edge_bias, edge_source, boundary, node_count, decoder_projection_weight, dec_source, dec_weight, state, target, area, var_weight):
    member_score_sum = N_MEMBER
    region_loss_sum = N_REGION
    pairwise_score_sum = member_score_sum * region_loss_sum
    feature_width = W
    rim_size = BND
    table_rows = NL + 2 * rim_size
    hidden = latent.reshape(member_score_sum, region_loss_sum, NL, feature_width)
    features = layer_norm(hidden, node_gain)
    region_ids = jnp.arange(region_loss_sum)[:, None]
    tables = with_rims(features, features[:, region_ids, boundary])
    w_key_value = w_qkv[:, feature_width:]

    def repeat(values):
        return jnp.broadcast_to(values[None], (member_score_sum,) + values.shape).reshape((pairwise_score_sum,) + values.shape[1:])

    def flatten(values):
        return values.reshape((pairwise_score_sum,) + values.shape[2:])
    biases = repeat(edge_bias.reshape(region_loss_sum, NL, HEADS * K))
    sources = repeat(edge_source.reshape(region_loss_sum, NL, K))
    live_mask = (jnp.arange(NL)[None, :] < node_count[:, None])[:, :, None]

    def project(node_table):
        queries = jnp.dot(node_table[:NL], w_qkv[:, :feature_width], preferred_element_type=jnp.float32).astype(jnp.bfloat16)
        key_value = jnp.dot(node_table, w_key_value, preferred_element_type=jnp.float32).astype(jnp.bfloat16)
        return (queries, key_value)

    def forward_node(inputs):
        node_table, own_rows, bias_rows, edge_src, live_rows = inputs
        queries, key_value = project(node_table)
        attended, kept_values = attend(queries, key_value, bias_rows, edge_src)
        update = own_rows.astype(jnp.float32) + jnp.dot(attended, w_out, preferred_element_type=jnp.float32)
        return jnp.where(live_rows, update, 0.0).astype(jnp.bfloat16)
    node_out = lax.map(forward_node, (flatten(tables), flatten(hidden), biases, sources, repeat(live_mask)))
    node_out = node_out.reshape(member_score_sum, region_loss_sum, NL, feature_width)
    grid_tables = with_rims(node_out, node_out[:, region_ids, boundary])
    decoder_sender = repeat(dec_source.reshape(NDEC, region_loss_sum, REGION_POINTS).transpose(1, 0, 2))
    decoder_edge_weight = repeat(dec_weight.reshape(NDEC, region_loss_sum, REGION_POINTS).transpose(1, 0, 2))

    def decode(inputs):
        grid_table, edge_src, edge_wt = inputs
        picked_rows = grid_table[edge_src]
        edge_signal = lax.optimization_barrier(jnp.sum(edge_wt[:, :, None] * picked_rows.astype(jnp.float32), axis=0)).astype(jnp.bfloat16)
        increment = lax.dot_general(decoder_projection_weight, edge_signal, (((0,), (1,)), ((), ())), preferred_element_type=jnp.float32)
        return (edge_signal, increment)
    edge_signals, state_deltas = lax.map(decode, (flatten(grid_tables), decoder_sender, decoder_edge_weight))
    hidden_state_rows = state.reshape(OUTPUT_VARIABLES, region_loss_sum, REGION_POINTS).transpose(1, 0, 2)
    target_rows = target.reshape(OUTPUT_VARIABLES, region_loss_sum, REGION_POINTS).transpose(1, 0, 2)
    predicted_fields = hidden_state_rows[None] + state_deltas.reshape(member_score_sum, region_loss_sum, OUTPUT_VARIABLES, REGION_POINTS)
    weight_factor = area.reshape(region_loss_sum, REGION_POINTS)[:, None, :] * var_weight[None, :, None] / OUTPUT_VARIABLES
    region_wise_output = predicted_fields.transpose(1, 0, 2, 3)
    partials, gradient_collection = jax.vmap(ensemble_score_parts)(region_wise_output, region_wise_output, target_rows, weight_factor)
    loss = jnp.sum(partials) / GRID
    prediction_gradient = gradient_collection.transpose(1, 0, 2, 3).reshape(pairwise_score_sum, OUTPUT_VARIABLES, REGION_POINTS)

    def decoder_reverse_pass(carry, inputs):
        edge_signal, grad_rows, edge_src, edge_wt = inputs
        carry = carry + lax.dot_general(edge_signal, grad_rows, (((0,), (1,)), ((), ())), preferred_element_type=jnp.float32)
        grad_message = lax.dot_general(grad_rows, decoder_projection_weight, (((0,), (1,)), ((), ())), preferred_element_type=jnp.float32)
        spread_rows = (edge_wt[:, :, None] * grad_message[None]).reshape(-1, feature_width)
        grad_table = jax.ops.segment_sum(spread_rows, edge_src.reshape(-1), num_segments=table_rows)
        return (carry, grad_table)
    decoder_weight_gradient, gradient_lookup_tables = lax.scan(decoder_reverse_pass, jnp.zeros((feature_width, OUTPUT_VARIABLES), jnp.float32), (edge_signals, prediction_gradient, decoder_sender, decoder_edge_weight))
    gradient_lookup_tables = gradient_lookup_tables.reshape(member_score_sum, region_loss_sum, table_rows, feature_width)
    grad_node = gradient_lookup_tables[:, :, :NL].at[:, region_ids, boundary].add(rims_back(gradient_lookup_tables[:, :, NL:]))
    grad_node = jnp.where(live_mask[None], grad_node, 0.0)

    def processor_back(carry, inputs):
        grad_qkv_sum, grad_out_sum = carry
        node_table, grad_rows, bias_rows, edge_src = inputs
        grad_rows_b = grad_rows.astype(jnp.bfloat16)
        queries, key_value = project(node_table)
        attended, kept_values = attend(queries, key_value, bias_rows, edge_src)
        grad_out_sum = grad_out_sum + lax.dot_general(attended, grad_rows_b, (((0,), (0,)), ((), ())), preferred_element_type=jnp.float32)
        grad_mixed = lax.dot_general(grad_rows_b, w_out, (((1,), (1,)), ((), ())), preferred_element_type=jnp.float32).astype(jnp.bfloat16)
        grad_query, grad_key_value = attend_backward(grad_mixed, kept_values, edge_src, table_rows)
        grad_q = lax.dot_general(node_table[:NL], grad_query, (((0,), (0,)), ((), ())), preferred_element_type=jnp.float32)
        grad_kv = lax.dot_general(node_table, grad_key_value, (((0,), (0,)), ((), ())), preferred_element_type=jnp.float32)
        grad_qkv_sum = grad_qkv_sum + jnp.concatenate([grad_q, grad_kv], axis=1)
        own_grads = jnp.concatenate([grad_query, grad_key_value[:NL]], axis=1)
        grad_own = lax.dot_general(own_grads, w_qkv, (((1,), (1,)), ((), ())), preferred_element_type=jnp.float32)
        grad_rim = lax.dot_general(grad_key_value[NL:], w_key_value, (((1,), (1,)), ((), ())), preferred_element_type=jnp.float32)
        return ((grad_qkv_sum, grad_out_sum), (grad_own, grad_rim))
    start_sums = (jnp.zeros((feature_width, 3 * feature_width), jnp.float32), jnp.zeros((feature_width, feature_width), jnp.float32))
    (grad_qkv, grad_out), (grad_own, grad_rim) = lax.scan(processor_back, start_sums, (flatten(tables), flatten(grad_node), biases, sources))
    grad_own = grad_own.reshape(member_score_sum, region_loss_sum, NL, feature_width)
    grad_rim = grad_rim.reshape(member_score_sum, region_loss_sum, 2 * rim_size, feature_width)
    grad_features = grad_own.at[:, region_ids, boundary].add(rims_back(grad_rim))
    grad_latent = (grad_node + norm_backward(hidden, node_gain, grad_features)).astype(jnp.bfloat16)
    grad_latent = grad_latent.reshape(member_score_sum, NODES, feature_width)
    return (loss, grad_qkv, grad_out, decoder_weight_gradient, grad_latent)
```

```python
import functools
import math

import jax
import jax.numpy as jnp
from jax import lax
from jax.experimental import pallas as pl
from jax.experimental.pallas import tpu as pltpu
from jax.sharding import PartitionSpec as P

ALPHA = 0.95
NORM_EPS = 1e-05
SMOOTH_SQ = 0.25
SMOOTH_ROOT = 0.5
F32 = jnp.float32
BF16 = jnp.bfloat16
LANES = 128


def nn(left, right):
    return lax.dot_general(left, right, (((1,), (0,)), ((), ())), preferred_element_type=F32)


def nt(left, right):
    return lax.dot_general(left, right, (((1,), (1,)), ((), ())), preferred_element_type=F32)


def tn(left, right):
    return lax.dot_general(left, right, (((0,), (0,)), ((), ())), preferred_element_type=F32)


def on_core(name, kernel, outs, *args, scalars=(), scratch=()):
    return pl.pallas_call(
        kernel,
        name=name,
        out_shape=[jax.ShapeDtypeStruct(s, d) for s, d in outs],
        in_specs=[pl.BlockSpec(memory_space=pltpu.SMEM)] * len(scalars)
        + [pl.BlockSpec(memory_space=pltpu.VMEM)] * len(args),
        out_specs=[pl.BlockSpec(memory_space=pltpu.VMEM)] * len(outs),
        scratch_shapes=list(scratch),
        compiler_params=pltpu.CompilerParams(vmem_limit_bytes=48 * 1024 * 1024),
    )(*scalars, *args)


def iota(shape, dim):
    return lax.broadcasted_iota(jnp.int32, shape, dim)


def ones_where(mask):
    return jnp.where(mask, 1.0, 0.0).astype(BF16)


def shift_of(size):
    assert size & (size - 1) == 0
    return size.bit_length() - 1


def head_map(rows, cols, row_size, col_size):
    return ones_where(
        (iota((rows, cols), 0) >> shift_of(row_size)) == (iota((rows, cols), 1) >> shift_of(col_size))
    )


def group_reduce(values, size, op):
    lanes = values.shape[1]
    lane = iota(values.shape, 1)
    step = 1
    while step < size:
        partner = jnp.where(
            (lane & step) == 0,
            pltpu.roll(values, lanes - step, 1),
            pltpu.roll(values, step, 1),
        )
        values = op(values, partner)
        step *= 2
    return values


def norm_parts(hidden):
    values = hidden.astype(F32)
    center = values - jnp.mean(values, axis=-1, keepdims=True)
    inverse = lax.rsqrt(jnp.mean(center * center, axis=-1, keepdims=True) + NORM_EPS)
    return center * inverse, inverse


def picked(border_row, table):
    mask = ones_where(iota((table.shape[0], border_row.shape[1]), 0) == border_row)
    return tn(mask, table)


def norm_kernel(hidden_ref, gain_ref, border_ref, features_ref, head_ref, tail_ref):
    scaled, _ = norm_parts(hidden_ref[...])
    features = (scaled * gain_ref[...]).astype(BF16)
    features_ref[...] = features
    rows = picked(border_ref[...], features).astype(BF16)
    rim = head_ref.shape[0]
    head_ref[...] = rows[:rim]
    tail_ref[...] = rows[rim:]


def project_kernel(features_ref, w_ref, src_ref, weight_ref, q_ref, kv_ref, mix_ref):
    width = features_ref.shape[1]
    qkv = nn(features_ref[...], w_ref[...]).astype(BF16)
    q_ref[...] = qkv[:, :width]
    kv_ref[...] = qkv[:, width:]
    rows = iota(mix_ref.shape, 0)
    total = jnp.zeros(mix_ref.shape, F32)
    for j in range(src_ref.shape[0]):
        total += jnp.where(rows == src_ref[j : j + 1, :], weight_ref[j : j + 1, :], 0.0)
    mix_ref[...] = total.astype(BF16)


def attend_kernel(
    count_ref, hidden_ref, left_ref, right_ref, q_ref, kv_ref, w_ref, w_out_ref, bias_ref, src_ref,
    border_ref, out_ref, head_ref, tail_ref, probs_ref, attended_ref, keys_ref, values_ref, table_ref,
):
    nodes, width = hidden_ref.shape
    rim = left_ref.shape[0]
    edges = src_ref.shape[1]
    columns = bias_ref.shape[1]
    head_size = width // (columns // edges)
    w_kv = w_ref[:, width:]
    table_ref[:nodes] = kv_ref[...]
    table_ref[nodes : nodes + rim] = nn(left_ref[...], w_kv).astype(BF16)
    table_ref[nodes + rim :] = nn(right_ref[...], w_kv).astype(BF16)
    table = table_ref[...]
    queries = q_ref[...].astype(F32)
    squeeze = head_map(width, columns, head_size, edges)
    expand = head_map(columns, width, edges, head_size)
    lane = iota((nodes, columns), 1) & (edges - 1)
    slot = iota((nodes, table.shape[0]), 1)
    scores = jnp.zeros((nodes, columns), F32)
    for e in range(edges):
        rows = nn(ones_where(slot == src_ref[:, e : e + 1]), table)
        keys_ref[e] = rows[:, :width].astype(BF16)
        values_ref[e] = rows[:, width:].astype(BF16)
        part = nn((queries * rows[:, :width]).astype(BF16), squeeze)
        scores = jnp.where(lane == e, part, scores)
    scores = scores / math.sqrt(head_size) + bias_ref[...]
    shifted = jnp.exp(scores - group_reduce(scores, edges, jnp.maximum))
    probs = shifted / group_reduce(shifted, edges, jnp.add)
    probs_ref[...] = probs
    total = jnp.zeros((nodes, width), F32)
    for e in range(edges):
        share = nn(jnp.where(lane == e, probs, 0.0).astype(BF16), expand)
        total += share * values_ref[e].astype(F32)
    attended = total.astype(BF16)
    attended_ref[...] = attended
    update = hidden_ref[...].astype(F32) + nn(attended, w_out_ref[...])
    live = iota((nodes, width), 0) < count_ref[0]
    node_out = jnp.where(live, update, 0.0).astype(BF16)
    out_ref[...] = node_out
    rows = picked(border_ref[...], node_out).astype(BF16)
    head_ref[...] = rows[:rim]
    tail_ref[...] = rows[rim:]


def decode_kernel(
    own_ref, left_ref, right_ref, mix_ref, w_ref, message_ref, change_ref, sent_ref, table_ref
):
    nodes = own_ref.shape[0]
    rim = left_ref.shape[0]
    table_ref[:nodes] = own_ref[...]
    table_ref[nodes : nodes + rim] = left_ref[...]
    table_ref[nodes + rim :] = right_ref[...]
    message = tn(table_ref[...], mix_ref[...]).astype(BF16)
    message_ref[...] = message
    change = tn(w_ref[...], message)
    change_ref[...] = change
    sent_ref[...] = change.astype(BF16)


def smooth_root(values):
    return values * values + SMOOTH_SQ


def score_kernel(
    change_ref, every_ref, state_ref, target_ref, area_ref, var_ref, mix_ref, w_ref, rank_ref,
    grad_ref, message_ref, head_ref, tail_ref, loss_ref, *, points,
):
    members = every_ref.shape[0]
    fair = 1.0 - (1.0 - ALPHA) / members
    pair = fair / (2.0 * members * (members - 1))
    own = change_ref[...]
    variables = own.shape[0]
    spread = jnp.zeros_like(own)
    slope = jnp.zeros_like(own)
    me = rank_ref[0]
    for n in range(members):
        other = jnp.where(me == n, own, every_ref[n].astype(F32))
        gap = own - other
        square = smooth_root(gap)
        inverse = lax.rsqrt(square)
        spread += square * inverse - SMOOTH_ROOT
        slope += gap * inverse
    gap = state_ref[...] + own - target_ref[...]
    square = smooth_root(gap)
    inverse = lax.rsqrt(square)
    weight = area_ref[...] * var_ref[...] / variables
    term = (square * inverse - SMOOTH_ROOT) / members - pair * spread
    loss_ref[...] = jnp.full(loss_ref.shape, jnp.sum(term * weight) / points, F32)
    grad = ((gap * inverse / members - 2.0 * pair * slope) * weight).astype(BF16)
    grad_ref[...] = grad
    message = nn(w_ref[...], grad).astype(BF16)
    message_ref[...] = message
    rim = head_ref.shape[0]
    nodes = mix_ref.shape[0] - 2 * rim
    rows = nt(mix_ref[nodes:, :], message).astype(BF16)
    head_ref[...] = rows[:rim]
    tail_ref[...] = rows[rim:]


def score_call(rank, *args, outs, points):
    kernel = functools.partial(score_kernel, points=points)

    def ordered(rank_ref, change, every, state, target, area, var, mix, w, *out_refs):
        kernel(change, every, state, target, area, var, mix, w, rank_ref, *out_refs)

    return on_core("score", ordered, outs, *args, scalars=(rank,))


def own_rows_kernel(mix_ref, grad_message_ref, message_ref, grad_ref, own_ref, dec_ref):
    nodes = own_ref.shape[0]
    own_ref[...] = nt(mix_ref[:nodes, :], grad_message_ref[...])
    dec_ref[...] = nt(message_ref[...], grad_ref[...])


def node_grad_kernel(
    count_ref, own_ref, from_left_ref, from_right_ref, border_ref, attended_ref, w_out_ref,
    grad_ref, mixed_ref, out_ref, rows_ref,
):
    nodes, width = own_ref.shape
    rim = from_left_ref.shape[0]
    rows_ref[:rim] = from_left_ref[...]
    rows_ref[rim:] = from_right_ref[...]
    mask = ones_where(iota((nodes, 2 * rim), 0) == border_ref[...])
    total = own_ref[...] + nn(mask, rows_ref[...])
    total = jnp.where(iota((nodes, width), 0) < count_ref[0], total, 0.0)
    grad_ref[...] = total
    rounded = total.astype(BF16)
    mixed_ref[...] = nt(rounded, w_out_ref[...]).astype(BF16)
    out_ref[...] = tn(attended_ref[...], rounded)


def attend_back_kernel(
    mixed_ref, q_ref, probs_ref, keys_ref, values_ref, src_ref, w_ref,
    grad_query_ref, grad_kv_ref, head_ref, tail_ref, edge_ref, hot_ref,
):
    nodes, width = mixed_ref.shape
    edges = src_ref.shape[0]
    columns = probs_ref.shape[1]
    head_size = width // (columns // edges)
    inv_root = 1.0 / math.sqrt(head_size)
    squeeze = head_map(width, columns, head_size, edges)
    expand = head_map(columns, width, edges, head_size)
    lane = iota((nodes, columns), 1) & (edges - 1)
    mixed = mixed_ref[...].astype(F32)
    probs = probs_ref[...]
    grad_probs = jnp.zeros((nodes, columns), F32)
    for e in range(edges):
        part = nn((mixed * values_ref[e].astype(F32)).astype(BF16), squeeze)
        grad_probs = jnp.where(lane == e, part, grad_probs)
    grad_scores = probs * (grad_probs - group_reduce(probs * grad_probs, edges, jnp.add))
    query = q_ref[...].astype(F32) * inv_root
    total = jnp.zeros((nodes, width), F32)
    table_rows = hot_ref.shape[0]
    slot = iota((table_rows, nodes), 0)
    for e in range(edges):
        at = pl.ds(e * nodes, nodes)
        hot_ref[:, at] = ones_where(slot == src_ref[e : e + 1, :])
        share = nn(jnp.where(lane == e, grad_scores, 0.0).astype(BF16), expand)
        total += share * keys_ref[e].astype(F32)
        edge_ref[at, :width] = (share * query).astype(BF16)
        share = nn(jnp.where(lane == e, probs, 0.0).astype(BF16), expand)
        edge_ref[at, width:] = (share * mixed).astype(BF16)
    grad_query_ref[...] = (total * inv_root).astype(BF16)
    grad_kv = nn(hot_ref[...], edge_ref[...]).astype(BF16)
    grad_kv_ref[...] = grad_kv
    rim = head_ref.shape[0]
    rows = nt(grad_kv[nodes:], w_ref[:, width:]).astype(BF16)
    head_ref[...] = rows[:rim]
    tail_ref[...] = rows[rim:]


def split_rows(bits_ref, which, source, send_ref, keep_ref):
    mine = bits_ref[which]
    for i in range(send_ref.shape[0]):
        send_ref[i] = source[i, 1 - mine].astype(BF16)
        keep_ref[i] = source[i, mine]


def weight_grad_kernel(
    bits_ref, features_ref, left_ref, right_ref, grad_query_ref, grad_kv_ref, out_ref, dec_ref,
    loss_ref, send_ref, keep_ref, full_ref,
):
    nodes, width = features_ref.shape
    rim = left_ref.shape[0]
    variables = dec_ref.shape[1]
    pairs, _, rows, _ = full_ref.shape
    shape = (pairs, 2, rows)
    features = features_ref[...]

    def put(start, values):
        full_ref[:, :, :, start : start + values.shape[1]] = values.reshape(*shape, values.shape[1])

    put(0, tn(features, grad_query_ref[...]))
    total = tn(features, grad_kv_ref[:nodes, :])
    total += tn(left_ref[...], grad_kv_ref[nodes : nodes + rim, :])
    total += tn(right_ref[...], grad_kv_ref[nodes + rim :, :])
    put(width, total)
    put(3 * width, out_ref[...])
    dec = dec_ref[...]
    pad = jnp.concatenate([dec, jnp.zeros((width, LANES - variables), F32)], axis=1)
    loss = jnp.broadcast_to(loss_ref[0:1, 0:1], (width, LANES))
    high = loss.astype(BF16).astype(F32)
    lane = iota((width, LANES), 1)
    pad = jnp.where(lane == variables, high, pad)
    pad = jnp.where(lane == variables + 1, loss - high, pad)
    put(4 * width, pad)
    split_rows(bits_ref, 0, full_ref, send_ref, keep_ref)


def joined(keep, arrived, variables):
    total = keep + arrived.astype(F32)
    last = total[..., -LANES:]
    lane = iota(last.shape, last.ndim - 1)
    loss = last[..., variables : variables + 1] + last[..., variables + 1 : variables + 2]
    high = loss.astype(BF16).astype(F32)
    last = jnp.where(lane == variables, high, last)
    last = jnp.where(lane == variables + 1, loss - high, last)
    return total[..., :-LANES], last


def combine_kernel(bits_ref, keep_in_ref, arrived_ref, send_ref, keep_ref, *, which, variables):
    mine = bits_ref[which]
    for i in range(send_ref.shape[0]):
        for half in (0, 1):
            at = mine if half else 1 - mine
            body, last = joined(keep_in_ref[i, at], arrived_ref[i, at], variables)
            to = keep_ref if half else send_ref
            to[i, :, :-LANES] = body.astype(to.dtype)
            to[i, :, -LANES:] = last.astype(to.dtype)


def last_kernel(keep_ref, arrived_ref, sum_ref, *, variables):
    body, last = joined(keep_ref[...], arrived_ref[...], variables)
    sum_ref[:, :-LANES] = body.astype(BF16)
    sum_ref[:, -LANES:] = last.astype(BF16)


def unpack_kernel(sums_ref, qkv_ref, out_ref, dec_ref, loss_ref):
    width = out_ref.shape[1]
    variables = dec_ref.shape[1]
    qkv_ref[...] = sums_ref[:, : 3 * width].astype(F32)
    out_ref[...] = sums_ref[:, 3 * width : 4 * width].astype(F32)
    last = sums_ref[:, 4 * width :].astype(F32)
    dec_ref[...] = last[:, :variables]
    loss = last[0:1, variables : variables + 1] + last[0:1, variables + 1 : variables + 2]
    loss_ref[...] = jnp.broadcast_to(loss, loss_ref.shape)


def own_feature_kernel(grad_query_ref, grad_kv_ref, w_ref, grad_ref):
    nodes, width = grad_query_ref.shape
    grad_ref[...] = nt(grad_query_ref[...], w_ref[:, :width]) + nt(
        grad_kv_ref[:nodes, :], w_ref[:, width:]
    )


def latent_grad_kernel(
    hidden_ref, gain_ref, own_ref, from_left_ref, from_right_ref, border_ref, node_ref, grad_ref, rows_ref
):
    nodes = hidden_ref.shape[0]
    rim = from_left_ref.shape[0]
    rows_ref[:rim] = from_left_ref[...]
    rows_ref[rim:] = from_right_ref[...]
    mask = ones_where(iota((nodes, 2 * rim), 0) == border_ref[...])
    grad_rows = own_ref[...] + nn(mask, rows_ref[...])
    scaled, inverse = norm_parts(hidden_ref[...])
    scaled_grad = grad_rows * gain_ref[...]
    back = inverse * (
        scaled_grad
        - jnp.mean(scaled_grad, axis=-1, keepdims=True)
        - scaled * jnp.mean(scaled_grad * scaled, axis=-1, keepdims=True)
    )
    grad_ref[...] = (node_ref[...] + back).astype(BF16)


def swap_rims(head, tail):
    count = lax.axis_size("region")
    from_left = lax.ppermute(tail, "region", [(i, (i + 1) % count) for i in range(count)])
    from_right = lax.ppermute(head, "region", [((i + 1) % count, i) for i in range(count)])
    return from_left, from_right


def exchange_order(regions, members):
    order = [("member", 1 << b) for b in range(shift_of(members))]
    bits = [1 << b for b in range(shift_of(regions))]
    return order + [("region", b) for b in bits[:1] + bits[:0:-1]]


def body(
    latent,
    node_gain,
    w_qkv,
    w_out,
    edge_bias,
    edge_source,
    boundary,
    node_count,
    decoder_projection_weight,
    dec_source,
    dec_weight,
    state,
    target,
    area,
    var_weight,
):
    hidden = latent[0]
    nodes, width = hidden.shape
    rim = boundary.shape[1] // 2
    table_rows = nodes + 2 * rim
    edges = edge_source.shape[1]
    columns = edge_bias.shape[1]
    variables, points = state.shape
    regions, members = lax.axis_size("region"), lax.axis_size("member")
    total_points = points * regions
    gain = node_gain[None]
    rim_rows = ((rim, width), BF16)
    order = exchange_order(regions, members)
    where = {"region": lax.axis_index("region"), "member": lax.axis_index("member")}
    bits = jnp.stack([(where[axis] & bit) // bit for axis, bit in order]).astype(jnp.int32)
    rank = where["member"].astype(jnp.int32)[None]

    features, head, tail = on_core(
        "norm", norm_kernel, [((nodes, width), BF16), rim_rows, rim_rows], hidden, gain, boundary
    )
    left, right = swap_rims(head, tail)
    queries, own_kv, mix = on_core(
        "project",
        project_kernel,
        [((nodes, width), BF16), ((nodes, 2 * width), BF16), ((table_rows, points), BF16)],
        features, w_qkv, dec_source, dec_weight,
    )
    edge_rows = ((edges, nodes, width), BF16)
    node_out, head, tail, probs, attended, keys, values = on_core(
        "attend",
        attend_kernel,
        [
            ((nodes, width), BF16), rim_rows, rim_rows, ((nodes, columns), F32),
            ((nodes, width), BF16), edge_rows, edge_rows,
        ],
        hidden, left, right, queries, own_kv, w_qkv, w_out, edge_bias, edge_source, boundary,
        scalars=(node_count,),
        scratch=[pltpu.VMEM((table_rows, 2 * width), BF16)],
    )
    out_left, out_right = swap_rims(head, tail)
    message, change, sent = on_core(
        "decode",
        decode_kernel,
        [((width, points), BF16), ((variables, points), F32), ((variables, points), BF16)],
        node_out, out_left, out_right, mix, decoder_projection_weight,
        scratch=[pltpu.VMEM((table_rows, width), BF16)],
    )
    every = lax.all_gather(sent[None], "member", axis=0, tiled=True)
    grad, grad_message, head, tail, loss = score_call(
        rank, change, every, state, target, area[None], var_weight[:, None], mix,
        decoder_projection_weight,
        outs=[
            ((variables, points), BF16), ((width, points), BF16), rim_rows, rim_rows, ((8, LANES), F32),
        ],
        points=total_points,
    )
    back_left, back_right = swap_rims(head, tail)
    grad_own, grad_dec = on_core(
        "own_rows",
        own_rows_kernel,
        [((nodes, width), F32), ((width, variables), F32)],
        mix, grad_message, message, grad,
    )
    grad_node, grad_mixed, grad_out = on_core(
        "node_grad",
        node_grad_kernel,
        [((nodes, width), F32), ((nodes, width), BF16), ((width, width), F32)],
        grad_own, back_left, back_right, boundary, attended, w_out,
        scalars=(node_count,),
        scratch=[pltpu.VMEM((2 * rim, width), BF16)],
    )
    grad_query, grad_kv, head, tail = on_core(
        "attend_back",
        attend_back_kernel,
        [((nodes, width), BF16), ((table_rows, 2 * width), BF16), rim_rows, rim_rows],
        grad_mixed, queries, probs, keys, values, edge_source.T, w_qkv,
        scratch=[
            pltpu.VMEM((edges * nodes, 2 * width), BF16), pltpu.VMEM((table_rows, edges * nodes), BF16),
        ],
    )
    rim_left, rim_right = swap_rims(head, tail)

    packed = 4 * width + LANES
    rows = width // (regions * members)
    held = width // 2
    full = (held // rows, 2, rows, packed)
    half = (held // rows, rows, packed)
    send, keep = on_core(
        "weight_grad",
        weight_grad_kernel,
        [(half, BF16), (half, F32)],
        features, left, right, grad_query, grad_kv, grad_out, grad_dec, loss,
        scalars=(bits,),
        scratch=[pltpu.VMEM(full, F32)],
    )
    (own_feature,) = on_core(
        "own_feature", own_feature_kernel, [((nodes, width), F32)], grad_query, grad_kv, w_qkv
    )
    (grad_latent,) = on_core(
        "latent_grad",
        latent_grad_kernel,
        [((nodes, width), BF16)],
        hidden, gain, own_feature, rim_left, rim_right, boundary, grad_node,
        scratch=[pltpu.VMEM((2 * rim, width), BF16)],
    )

    kept_bits = []
    for axis, count in (("region", regions), ("member", members)):
        kept_bits += [(axis, 1 << b) for b in reversed(range(shift_of(count)))]
    for step, (axis, bit) in enumerate(order):
        count = lax.axis_size(axis)
        arrived = lax.ppermute(send, axis, [(i, i ^ bit) for i in range(count)])
        kept_bits.remove((axis, bit))
        if step + 1 == len(order):
            (total,) = on_core(
                "last", functools.partial(last_kernel, variables=variables),
                [((rows, packed), BF16)], keep.reshape(rows, packed), arrived.reshape(rows, packed),
            )
            break
        place = kept_bits.index(order[step + 1])
        before = 1 << place
        after = 1 << (len(kept_bits) - 1 - place)
        view = (before, 2, after * rows, packed)
        half = (before, after * rows, packed)
        send, keep = on_core(
            f"combine{step}",
            functools.partial(combine_kernel, which=step + 1, variables=variables),
            [(half, BF16), (half, F32)],
            keep.reshape(view), arrived.reshape(view),
            scalars=(bits,),
        )
    sums = lax.all_gather(total, "member", axis=0, tiled=True)
    held = sums.shape[0]
    share_qkv, share_out, share_dec, loss = on_core(
        "unpack",
        unpack_kernel,
        [((held, 3 * width), F32), ((held, width), F32), ((held, variables), F32), ((8, LANES), F32)],
        sums,
    )
    return (loss[0, 0], share_qkv, share_out, share_dec, grad_latent[None])


def solution(mesh):
    placed = (
        P("member", "region", None),
        P(),
        P(),
        P(),
        P("region", None),
        P("region", None),
        P("region", None),
        P("region"),
        P(),
        P(None, "region"),
        P(None, "region"),
        P(None, "region"),
        P(None, "region"),
        P("region"),
        P(),
    )
    return jax.shard_map(
        body,
        mesh=mesh,
        in_specs=placed,
        out_specs=(
            P(),
            P("region", None),
            P("region", None),
            P("region", None),
            P("member", "region", None),
        ),
        check_vma=False,
    )
```

```python
import functools
import math

import jax
import jax.numpy as jnp
from jax import lax
from jax.experimental import pallas as pl
from jax.experimental.pallas import tpu as pltpu
from jax.sharding import PartitionSpec as P


ALPHA = 0.95
NORM_EPS = 1e-05
SMOOTH_SQ = 0.25
SMOOTH_ROOT = 0.5
F32 = jnp.float32
BF16 = jnp.bfloat16
LANES = 128


def nn(left, right):
    return lax.dot_general(left, right, (((1,), (0,)), ((), ())), preferred_element_type=F32)


def nt(left, right):
    return lax.dot_general(left, right, (((1,), (1,)), ((), ())), preferred_element_type=F32)


def tn(left, right):
    return lax.dot_general(left, right, (((0,), (0,)), ((), ())), preferred_element_type=F32)


def on_core(kernel, outs, *args, fetched=0, scratch=(), mib=8):
    return pl.pallas_call(
        kernel,
        out_shape=[jax.ShapeDtypeStruct(s, d) for s, d in outs],
        in_specs=[pl.BlockSpec(memory_space=pltpu.HBM)] * fetched
        + [pl.BlockSpec(memory_space=pltpu.VMEM)] * (len(args) - fetched),
        out_specs=[pl.BlockSpec(memory_space=pltpu.VMEM)] * len(outs),
        scratch_shapes=list(scratch) + [pltpu.SemaphoreType.DMA((fetched,))] * (fetched > 0),
        compiler_params=pltpu.CompilerParams(vmem_limit_bytes=mib * 1024 * 1024),
    )(*[pltpu.with_memory_space_constraint(a, pltpu.HBM) for a in args[:fetched]], *args[fetched:])


def iota(shape, dim):
    return lax.broadcasted_iota(jnp.int32, shape, dim)


def ones_where(mask):
    return jnp.where(mask, 1.0, 0.0).astype(BF16)


def shift_of(size):
    assert size & (size - 1) == 0
    return size.bit_length() - 1


def head_map(rows, cols, row_size, col_size):
    return ones_where(
        (iota((rows, cols), 0) >> shift_of(row_size)) == (iota((rows, cols), 1) >> shift_of(col_size))
    )


def group_reduce(values, size, op):
    lanes = values.shape[1]
    lane = iota(values.shape, 1)
    step = 1
    while step < size:
        partner = jnp.where(
            (lane & step) == 0,
            pltpu.roll(values, lanes - step, 1),
            pltpu.roll(values, step, 1),
        )
        values = op(values, partner)
        step *= 2
    return values


def norm_parts(hidden):
    values = hidden.astype(F32)
    center = values - jnp.mean(values, axis=-1, keepdims=True)
    inverse = lax.rsqrt(jnp.mean(center * center, axis=-1, keepdims=True) + NORM_EPS)
    return center * inverse, inverse


def bit_of(axis, bit):
    return (lax.axis_index(axis) >> shift_of(bit)) & 1


def border_map(border_ref, nodes):
    return ones_where(iota((nodes, border_ref.shape[1]), 0) == border_ref[...])


def fetch(pairs, sems):
    copies = [pltpu.make_async_copy(a, b, sems.at[i]) for i, (a, b) in enumerate(pairs)]
    for copy in copies:
        copy.start()
    return copies


def norm_kernel(
    hidden_hbm, gain_hbm, border_hbm, features_ref, head_ref, tail_ref, hidden_ref, gain_ref, border_ref, sems
):
    pairs = ((hidden_hbm, hidden_ref), (gain_hbm, gain_ref), (border_hbm, border_ref))
    for copy in fetch(pairs, sems):
        copy.wait()
    scaled, _ = norm_parts(hidden_ref[...])
    features = (scaled * gain_ref[...]).astype(BF16)
    features_ref[...] = features
    rows = tn(border_map(border_ref, features.shape[0]), features).astype(BF16)
    rim = head_ref.shape[0]
    head_ref[...] = rows[:rim]
    tail_ref[...] = rows[rim:]


def project_kernel(
    w_hbm, src_hbm, weight_hbm, features_ref, q_ref, kv_ref, mix_ref, w_ref, src_ref, weight_ref, sems
):
    copies = fetch(((src_hbm, src_ref), (weight_hbm, weight_ref), (w_hbm, w_ref)), sems)
    width = features_ref.shape[1]
    rows = iota(mix_ref.shape, 0)
    copies[0].wait()
    copies[1].wait()
    total = jnp.zeros(mix_ref.shape, F32)
    for j in range(src_ref.shape[0]):
        total += jnp.where(rows == src_ref[j : j + 1, :], weight_ref[j : j + 1, :], 0.0)
    mix_ref[...] = total.astype(BF16)
    copies[2].wait()
    qkv = nn(features_ref[...], w_ref[...]).astype(BF16)
    q_ref[...] = qkv[:, :width]
    kv_ref[...] = qkv[:, width:]


def attend_kernel(
    w_out_hbm, bias_hbm, dec_hbm, count_ref, hidden_ref, left_ref, right_ref, q_ref, kv_ref, w_ref,
    src_ref, border_ref, out_ref, projected_ref, head_ref, tail_ref, probs_ref, attended_ref, keys_ref, values_ref, table_ref,
    w_out_ref, bias_ref, dec_ref, sems,
):
    copies = fetch(((bias_hbm, bias_ref), (w_out_hbm, w_out_ref), (dec_hbm, dec_ref)), sems)
    nodes, width = hidden_ref.shape
    rim = left_ref.shape[0]
    edges = src_ref.shape[0]
    columns = bias_ref.shape[1]
    sources = src_ref[...].astype(F32).T
    head_size = width // (columns // edges)
    w_kv = w_ref[:, width:]
    table_ref[:nodes] = kv_ref[...]
    table_ref[nodes : nodes + rim] = nn(left_ref[...], w_kv).astype(BF16)
    table_ref[nodes + rim :] = nn(right_ref[...], w_kv).astype(BF16)
    table = table_ref[...]
    queries = q_ref[...].astype(F32)
    squeeze = head_map(width, columns, head_size, edges)
    expand = head_map(columns, width, edges, head_size)
    lane = iota((nodes, columns), 1) & (edges - 1)
    slot = iota((nodes, table.shape[0]), 1).astype(F32)
    scores = jnp.zeros((nodes, columns), F32)
    for e in range(edges):
        rows = nn(ones_where(slot == sources[:, e : e + 1]), table)
        keys_ref[e] = rows[:, :width].astype(BF16)
        values_ref[e] = rows[:, width:].astype(BF16)
        part = nn((queries * rows[:, :width]).astype(BF16), squeeze)
        scores = jnp.where(lane == e, part, scores)
    copies[0].wait()
    scores = scores / math.sqrt(head_size) + bias_ref[...]
    shifted = jnp.exp(scores - group_reduce(scores, edges, jnp.maximum))
    probs = shifted / group_reduce(shifted, edges, jnp.add)
    probs_ref[...] = probs
    total = jnp.zeros((nodes, width), F32)
    for e in range(edges):
        share = nn(jnp.where(lane == e, probs, 0.0).astype(BF16), expand)
        total += share * values_ref[e].astype(F32)
    attended = total.astype(BF16)
    attended_ref[...] = attended
    copies[1].wait()
    update = hidden_ref[...].astype(F32) + nn(attended, w_out_ref[...])
    live = iota((nodes, width), 0) < count_ref[...]
    node_out = jnp.where(live, update, 0.0).astype(BF16)
    out_ref[...] = node_out
    copies[2].wait()
    projected = nt(dec_ref[...], node_out).astype(BF16)
    projected_ref[...] = projected
    columns = nn(projected, border_map(border_ref, nodes)).astype(BF16)
    head_ref[...] = columns[:, :rim]
    tail_ref[...] = columns[:, rim:]


def decode_kernel(own_ref, left_ref, right_ref, mix_ref, change_ref, sent_ref):
    table = jnp.concatenate([own_ref[...], left_ref[...], right_ref[...]], axis=1)
    change = nn(table, mix_ref[...])
    change_ref[...] = change
    sent_ref[...] = change.astype(BF16)


def smooth_root(values):
    return values * values + SMOOTH_SQ


def score_kernel(
    change_ref, every_ref, state_ref, target_ref, area_ref, var_ref, mix_ref,
    grad_ref, head_ref, tail_ref, loss_ref, *, points,
):
    members = every_ref.shape[0]
    fair = 1.0 - (1.0 - ALPHA) / members
    pair = fair / (2.0 * members * (members - 1))
    own = change_ref[...]
    variables = own.shape[0]
    spread = jnp.zeros_like(own)
    slope = jnp.zeros_like(own)
    me = lax.axis_index("member")
    for n in range(members):
        other = jnp.where(me == n, own, every_ref[n].astype(F32))
        gap = own - other
        square = smooth_root(gap)
        inverse = lax.rsqrt(square)
        spread += square * inverse - SMOOTH_ROOT
        slope += gap * inverse
    gap = state_ref[...] + own - target_ref[...]
    square = smooth_root(gap)
    inverse = lax.rsqrt(square)
    square_map = (variables, variables)
    diagonal = iota(square_map, 0) == iota(square_map, 1)
    var = jnp.sum(jnp.where(diagonal, var_ref[...], 0.0), axis=1, keepdims=True)
    weight = area_ref[...] * var / variables
    term = (square * inverse - SMOOTH_ROOT) / members - pair * spread
    loss_ref[...] = jnp.full(loss_ref.shape, jnp.sum(term * weight) / points, F32)
    grad = ((gap * inverse / members - 2.0 * pair * slope) * weight).astype(BF16)
    grad_ref[...] = grad
    rim = head_ref.shape[1]
    nodes = mix_ref.shape[0] - 2 * rim
    columns = nt(grad, mix_ref[nodes:, :]).astype(BF16)
    head_ref[...] = columns[:, :rim]
    tail_ref[...] = columns[:, rim:]


def own_rows_kernel(mix_ref, grad_ref, src_ref, own_ref, hot_ref):
    nodes = own_ref.shape[1]
    own_ref[...] = nt(grad_ref[...], mix_ref[:nodes, :])
    slot = iota((hot_ref.shape[0], nodes), 0)
    for e in range(src_ref.shape[0]):
        hot_ref[:, e * nodes : (e + 1) * nodes] = ones_where(slot == src_ref[e : e + 1, :])


def split_halves(mine, source_ref, send_ref, keep_ref):
    for i in range(send_ref.shape[0]):
        send_ref[i] = source_ref[i, 1 - mine].astype(BF16)
        keep_ref[i] = source_ref[i, mine]


def put(full_ref, start, values):
    shape = full_ref.shape[:3]
    full_ref[:, :, :, start : start + values.shape[1]] = values.reshape(*shape, values.shape[1])


def value_back_kernel(
    count_ref, own_ref, from_left_ref, from_right_ref, border_ref, node_out_ref, w_dec_ref,
    attended_ref, w_out_ref, probs_ref, hot_ref, features_ref, left_ref, right_ref, loss_ref,
    grad_ref, mixed_ref, grad_value_ref, send_ref, keep_ref, edge_ref, full_ref,
):
    nodes, width = grad_ref.shape
    rim = left_ref.shape[0]
    columns = probs_ref.shape[1]
    edges = hot_ref.shape[1] // nodes
    head_size = width // (columns // edges)
    returned = jnp.concatenate([from_left_ref[...], from_right_ref[...]], axis=1)
    columns_grad = (own_ref[...] + nt(returned, border_map(border_ref, nodes))).astype(BF16)
    total = tn(columns_grad, w_dec_ref[...])
    total = jnp.where(iota((nodes, width), 0) < count_ref[...], total, 0.0)
    grad_ref[...] = total
    rounded = total.astype(BF16)
    mixed = nt(rounded, w_out_ref[...]).astype(BF16)
    mixed_ref[...] = mixed
    mixed = mixed.astype(F32)
    expand = head_map(columns, width, edges, head_size)
    lane = iota((nodes, columns), 1) & (edges - 1)
    probs = probs_ref[...]
    for e in range(edges):
        share = nn(jnp.where(lane == e, probs, 0.0).astype(BF16), expand)
        edge_ref[e * nodes : (e + 1) * nodes, :] = (share * mixed).astype(BF16)
    grad_value = nn(hot_ref[...], edge_ref[...]).astype(BF16)
    grad_value_ref[...] = grad_value
    features = features_ref[...]
    total = tn(features, grad_value[:nodes])
    total += tn(left_ref[...], grad_value[nodes : nodes + rim])
    total += tn(right_ref[...], grad_value[nodes + rim :])
    put(full_ref, 0, total)
    put(full_ref, width, tn(attended_ref[...], rounded))
    variables = columns_grad.shape[0]
    dec = nn(columns_grad, node_out_ref[...])
    pad = jnp.concatenate([dec, jnp.zeros((LANES - variables, width), F32)], axis=0).T
    loss = jnp.broadcast_to(loss_ref[0:1, 0:1], (width, LANES))
    high = loss.astype(BF16).astype(F32)
    lane = iota((width, LANES), 1)
    pad = jnp.where(lane == variables, high, pad)
    pad = jnp.where(lane == variables + 1, loss - high, pad)
    put(full_ref, 2 * width, pad)
    split_halves(bit_of("member", 1), full_ref, send_ref, keep_ref)


def score_back_kernel(mixed_ref, probs_ref, values_ref, grad_ref):
    nodes, width = mixed_ref.shape
    edges = values_ref.shape[0]
    columns = probs_ref.shape[1]
    squeeze = head_map(width, columns, width // (columns // edges), edges)
    lane = iota((nodes, columns), 1) & (edges - 1)
    mixed = mixed_ref[...].astype(F32)
    probs = probs_ref[...]
    grad_probs = jnp.zeros((nodes, columns), F32)
    for e in range(edges):
        part = nn((mixed * values_ref[e].astype(F32)).astype(BF16), squeeze)
        grad_probs = jnp.where(lane == e, part, grad_probs)
    grad_ref[...] = probs * (grad_probs - group_reduce(probs * grad_probs, edges, jnp.add))


def query_back_kernel(
    grad_scores_ref, q_ref, keys_ref, hot_ref, grad_value_ref, w_ref,
    grad_query_ref, grad_key_ref, head_ref, tail_ref, edge_ref,
):
    nodes, width = q_ref.shape
    edges = keys_ref.shape[0]
    columns = grad_scores_ref.shape[1]
    head_size = width // (columns // edges)
    inv_root = 1.0 / math.sqrt(head_size)
    expand = head_map(columns, width, edges, head_size)
    lane = iota((nodes, columns), 1) & (edges - 1)
    grad_scores = grad_scores_ref[...]
    query = q_ref[...].astype(F32) * inv_root
    total = jnp.zeros((nodes, width), F32)
    for e in range(edges):
        share = nn(jnp.where(lane == e, grad_scores, 0.0).astype(BF16), expand)
        total += share * keys_ref[e].astype(F32)
        edge_ref[e * nodes : (e + 1) * nodes, :] = (share * query).astype(BF16)
    grad_query_ref[...] = (total * inv_root).astype(BF16)
    grad_key = nn(hot_ref[...], edge_ref[...]).astype(BF16)
    grad_key_ref[...] = grad_key
    rim = head_ref.shape[0]
    rows = nt(grad_key[nodes:], w_ref[:, width : 2 * width])
    rows += nt(grad_value_ref[nodes:, :], w_ref[:, 2 * width :])
    rows = rows.astype(BF16)
    head_ref[...] = rows[:rim]
    tail_ref[...] = rows[rim:]


def query_weight_kernel(
    features_ref, left_ref, right_ref, grad_query_ref, grad_key_ref, send_ref, keep_ref, full_ref
):
    nodes, width = features_ref.shape
    rim = left_ref.shape[0]
    features = features_ref[...]
    put(full_ref, 0, tn(features, grad_query_ref[...]))
    total = tn(features, grad_key_ref[:nodes, :])
    total += tn(left_ref[...], grad_key_ref[nodes : nodes + rim, :])
    total += tn(right_ref[...], grad_key_ref[nodes + rim :, :])
    put(full_ref, width, total)
    split_halves(bit_of("member", 1), full_ref, send_ref, keep_ref)


def joined(keep, arrived, variables):
    total = keep.astype(F32) + arrived.astype(F32)
    if variables is None:
        return total
    last = total[..., -LANES:]
    lane = iota(last.shape, last.ndim - 1)
    loss = last[..., variables : variables + 1] + last[..., variables + 1 : variables + 2]
    high = loss.astype(BF16).astype(F32)
    last = jnp.where(lane == variables, high, last)
    last = jnp.where(lane == variables + 1, loss - high, last)
    return jnp.concatenate([total[..., :-LANES], last], axis=-1)


def combine_kernel(keep_in_ref, arrived_ref, send_ref, keep_ref, *, axis, bit, variables):
    mine = bit_of(axis, bit)
    for i in range(send_ref.shape[0]):
        away = 1 - mine
        send_ref[i] = joined(keep_in_ref[i, away], arrived_ref[i, away], variables).astype(BF16)
        keep_ref[i] = joined(keep_in_ref[i, mine], arrived_ref[i, mine], variables)


def merge_kernel(
    query_keep_ref, query_in_ref, value_keep_ref, value_in_ref, send_ref, keep_ref, *, axis, bit, variables
):
    mine = bit_of(axis, bit)
    start = query_keep_ref.shape[-1]
    for at, out_ref in ((1 - mine, send_ref), (mine, keep_ref)):
        for i in range(send_ref.shape[0]):
            query = joined(query_keep_ref[i, at], query_in_ref[i, at], None)
            value = joined(value_keep_ref[i, at], value_in_ref[i, at], variables)
            out_ref[i, :, :start] = query.astype(out_ref.dtype)
            out_ref[i, :, start:] = value.astype(out_ref.dtype)


def total_kernel(keep_ref, arrived_ref, sum_ref, *, variables):
    for i in range(sum_ref.shape[0]):
        sum_ref[i] = joined(keep_ref[i], arrived_ref[i], variables).astype(BF16)


def swapped(array, axis, bit):
    count = lax.axis_size(axis)
    return lax.ppermute(array, axis, [(i, i ^ bit) for i in range(count)])


class Halving:
    def __init__(self, regions, members, rows):
        self.left = [("region", 1 << b) for b in reversed(range(shift_of(regions)))]
        self.left += [("member", 1 << b) for b in reversed(range(shift_of(members)))]
        self.rows = rows

    def half(self, step, packed):
        place = self.left.index(step)
        half = (1 << place, (1 << (len(self.left) - 1 - place)) * self.rows, packed)
        return half, (half[0], 2) + half[1:]

    def run(self, send, keep, steps, variables):
        packed = send.shape[-1]
        for i, (axis, bit) in enumerate(steps):
            arrived = swapped(send, axis, bit)
            self.left.remove((axis, bit))
            if i + 1 == len(steps):
                return keep, arrived
            half, both = self.half(steps[i + 1], packed)
            send, keep = on_core(
                functools.partial(
                    combine_kernel, axis=steps[i + 1][0], bit=steps[i + 1][1], variables=variables
                ),
                [(half, BF16), (half, F32)],
                keep.reshape(both), arrived.reshape(both),
            )


def unpack_kernel(*refs, aways):
    sum_refs = refs[: len(aways)]
    qkv_ref, out_ref, dec_ref, loss_ref = refs[len(aways) :]
    width = out_ref.shape[-1]
    variables = dec_ref.shape[-1]
    place = lax.axis_index("member")
    for ref, away in zip(sum_refs, aways):
        at = place ^ away
        qkv_ref[at] = ref[:, : 3 * width].astype(F32)
        out_ref[at] = ref[:, 3 * width : 4 * width].astype(F32)
        dec_ref[at] = ref[:, 4 * width : 4 * width + variables].astype(F32)
    last = sum_refs[0][0:1, 4 * width :].astype(F32)
    loss_ref[...] = last[:, variables : variables + 1] + last[:, variables + 1 : variables + 2]


def own_feature_kernel(grad_query_ref, grad_key_ref, grad_value_ref, w_ref, grad_ref):
    nodes, width = grad_query_ref.shape
    total = nt(grad_query_ref[...], w_ref[:, :width])
    total += nt(grad_key_ref[:nodes, :], w_ref[:, width : 2 * width])
    grad_ref[...] = total + nt(grad_value_ref[:nodes, :], w_ref[:, 2 * width :])


def latent_grad_kernel(
    hidden_ref, gain_ref, own_ref, from_left_ref, from_right_ref, border_ref, node_ref, grad_ref, rows_ref
):
    nodes = hidden_ref.shape[0]
    rim = from_left_ref.shape[0]
    rows_ref[:rim] = from_left_ref[...]
    rows_ref[rim:] = from_right_ref[...]
    mask = ones_where(iota((nodes, 2 * rim), 0) == border_ref[...])
    grad_rows = own_ref[...] + nn(mask, rows_ref[...])
    scaled, inverse = norm_parts(hidden_ref[...])
    scaled_grad = grad_rows * gain_ref[...]
    back = inverse * (
        scaled_grad
        - jnp.mean(scaled_grad, axis=-1, keepdims=True)
        - scaled * jnp.mean(scaled_grad * scaled, axis=-1, keepdims=True)
    )
    grad_ref[...] = (node_ref[...] + back).astype(BF16)


def swap_rims(head, tail):
    count = lax.axis_size("region")
    from_left = lax.ppermute(tail, "region", [(i, (i + 1) % count) for i in range(count)])
    from_right = lax.ppermute(head, "region", [((i + 1) % count, i) for i in range(count)])
    return from_left, from_right


def layer(
    latent,
    node_gain,
    w_qkv,
    w_out,
    edge_bias,
    edge_source,
    boundary,
    node_count,
    decoder_projection_weight,
    dec_source,
    dec_weight,
    state,
    target,
    area,
    var_weight,
):
    hidden = latent[0]
    nodes, width = hidden.shape
    rim = boundary.shape[1] // 2
    table_rows = nodes + 2 * rim
    sources = edge_source.T
    edges = sources.shape[0]
    w_decoder = decoder_projection_weight.T
    count = node_count[None]
    columns = edge_bias.shape[1]
    variables, points = state.shape
    regions, members = lax.axis_size("region"), lax.axis_size("member")
    total_points = points * regions
    gain = node_gain[None]
    rim_rows = ((rim, width), BF16)
    rim_columns = ((variables, rim), BF16)
    features, head, tail = on_core(
        norm_kernel,
        [((nodes, width), BF16), rim_rows, rim_rows],
        hidden, gain, boundary,
        fetched=3,
        scratch=[
            pltpu.VMEM((nodes, width), BF16), pltpu.VMEM((1, width), F32), pltpu.VMEM((1, 2 * rim), jnp.int32),
        ],
        mib=4,
    )
    left, right = swap_rims(head, tail)
    queries, own_kv, mix, w_qkv = on_core(
        project_kernel,
        [
            ((nodes, width), BF16), ((nodes, 2 * width), BF16), ((table_rows, points), BF16),
            ((width, 3 * width), BF16),
        ],
        w_qkv, dec_source, dec_weight, features,
        fetched=3,
        scratch=[pltpu.VMEM(dec_source.shape, jnp.int32), pltpu.VMEM(dec_weight.shape, F32)],
    )
    edge_rows = ((edges, nodes, width), BF16)
    node_out, projected, head, tail, probs, attended, keys, values = on_core(
        attend_kernel,
        [
            ((nodes, width), BF16), ((variables, nodes), BF16), rim_columns, rim_columns,
            ((nodes, columns), F32), ((nodes, width), BF16), edge_rows, edge_rows,
        ],
        w_out, edge_bias, w_decoder, count, hidden, left, right, queries, own_kv, w_qkv, sources, boundary,
        fetched=3,
        scratch=[
            pltpu.VMEM((table_rows, 2 * width), BF16), pltpu.VMEM((width, width), BF16),
            pltpu.VMEM((nodes, columns), F32), pltpu.VMEM((variables, width), BF16),
        ],
        mib=16,
    )
    out_left, out_right = swap_rims(head, tail)
    change, sent = on_core(
        decode_kernel,
        [((variables, points), F32), ((variables, points), BF16)],
        projected, out_left, out_right, mix,
    )
    every = lax.all_gather(sent[None], "member", axis=0, tiled=True)
    grad, head, tail, loss = on_core(
        functools.partial(score_kernel, points=total_points),
        [((variables, points), BF16), rim_columns, rim_columns, ((1, LANES), F32)],
        change, every, state, target, area[None], var_weight[None], mix,
    )
    back_left, back_right = swap_rims(head, tail)
    grad_own, hot = on_core(
        own_rows_kernel,
        [((variables, nodes), F32), ((table_rows, edges * nodes), BF16)],
        mix, grad, sources,
    )
    rows = width // (regions * members)
    pieces = regions * members // 2

    def halves(packed):
        return [((pieces, rows, packed), BF16), ((pieces, rows, packed), F32)]

    def whole(packed):
        return pltpu.VMEM((pieces, 2, rows, packed), F32)

    grad_node, grad_mixed, grad_value, value_send, value_keep = on_core(
        value_back_kernel,
        [((nodes, width), F32), ((nodes, width), BF16), ((table_rows, width), BF16)]
        + halves(2 * width + LANES),
        count, grad_own, back_left, back_right, boundary, node_out, w_decoder,
        attended, w_out, probs, hot, features, left, right, loss,
        scratch=[pltpu.VMEM((edges * nodes, width), BF16), whole(2 * width + LANES)],
        mib=16,
    )
    (grad_scores,) = on_core(
        score_back_kernel, [((nodes, columns), F32)], grad_mixed, probs, values
    )
    grad_query, grad_key, head, tail = on_core(
        query_back_kernel,
        [((nodes, width), BF16), ((table_rows, width), BF16), rim_rows, rim_rows],
        grad_scores, queries, keys, hot, grad_value, w_qkv,
        scratch=[pltpu.VMEM((edges * nodes, width), BF16)],
        mib=12,
    )
    rim_left, rim_right = swap_rims(head, tail)
    query_send, query_keep = on_core(
        query_weight_kernel,
        halves(2 * width),
        features, left, right, grad_query, grad_key,
        scratch=[whole(2 * width)],
    )
    (own_feature,) = on_core(
        own_feature_kernel, [((nodes, width), F32)], grad_query, grad_key, grad_value, w_qkv
    )
    (grad_latent,) = on_core(
        latent_grad_kernel,
        [((nodes, width), BF16)],
        hidden, gain, own_feature, rim_left, rim_right, boundary, grad_node,
        scratch=[pltpu.VMEM((2 * rim, width), BF16)],
    )

    core = [("member", 1)]
    across = [("member", 1 << b) for b in range(1, shift_of(members))]
    around = [("region", 1 << b) for b in range(shift_of(regions))]
    value_sum, query_sum = Halving(regions, members, rows), Halving(regions, members, rows)
    value_keep, value_in = value_sum.run(
        value_send, value_keep, core + across + around[:2], variables
    )
    query_keep, query_in = query_sum.run(
        query_send, query_keep, core + across + around[1::-1], None
    )
    packed = 4 * width + LANES
    half, _ = value_sum.half(around[2], packed)
    _, both_values = value_sum.half(around[2], 2 * width + LANES)
    _, both_queries = value_sum.half(around[2], 2 * width)
    send, keep = on_core(
        functools.partial(merge_kernel, axis=around[2][0], bit=around[2][1], variables=variables),
        [(half, BF16), (half, F32)],
        query_keep.reshape(both_queries), query_in.reshape(both_queries),
        value_keep.reshape(both_values), value_in.reshape(both_values),
    )
    keep, arrived = value_sum.run(send, keep, around[2:], variables)
    piece = (1, rows, packed)
    (total,) = on_core(
        functools.partial(total_kernel, variables=variables), [(piece, BF16)],
        keep.reshape(piece), arrived.reshape(piece),
    )
    sums, aways = [total.reshape(rows, packed)], [0]
    for axis, bit in across[::-1] + core:
        sums = sums + [swapped(piece, axis, bit) for piece in sums]
        aways = aways + [away ^ bit for away in aways]
    share_qkv, share_out, share_dec, loss = on_core(
        functools.partial(unpack_kernel, aways=aways),
        [
            ((members, rows, 3 * width), F32), ((members, rows, width), F32),
            ((members, rows, variables), F32), ((1, 1), F32),
        ],
        *sums,
    )
    held = members * rows
    return (
        loss.reshape(()),
        share_qkv.reshape(held, 3 * width),
        share_out.reshape(held, width),
        share_dec.reshape(held, variables),
        grad_latent[None],
    )


def solution(mesh):
    placed = (
        P("member", "region", None),
        P(),
        P(),
        P(),
        P("region", None),
        P("region", None),
        P("region", None),
        P("region"),
        P(),
        P(None, "region"),
        P(None, "region"),
        P(None, "region"),
        P(None, "region"),
        P("region"),
        P(),
    )
    return jax.shard_map(
        layer,
        mesh=mesh,
        in_specs=placed,
        out_specs=(
            P(),
            P("region", None),
            P("region", None),
            P("region", None),
            P("member", "region", None),
        ),
        check_vma=False,
    )
```

```python
import functools
import math

import jax
import jax.numpy as jnp
from jax import lax
from jax.experimental import pallas as pl
from jax.experimental.pallas import tpu as pltpu
from jax.sharding import PartitionSpec as P


ALPHA = 0.95
NORM_EPS = 1e-05
SMOOTH_SQ = 0.25
SMOOTH_ROOT = 0.5
F32 = jnp.float32
BF16 = jnp.bfloat16
LANES = 128


def nn(left, right):
    return lax.dot_general(left, right, (((1,), (0,)), ((), ())), preferred_element_type=F32)


def nt(left, right):
    return lax.dot_general(left, right, (((1,), (1,)), ((), ())), preferred_element_type=F32)


def tn(left, right):
    return lax.dot_general(left, right, (((0,), (0,)), ((), ())), preferred_element_type=F32)


def on_core(kernel, outs, *args, fetched=0, scratch=(), mib=8):
    return pl.pallas_call(
        kernel,
        out_shape=[jax.ShapeDtypeStruct(s, d) for s, d in outs],
        in_specs=[pl.BlockSpec(memory_space=pltpu.HBM)] * fetched
        + [pl.BlockSpec(memory_space=pltpu.VMEM)] * (len(args) - fetched),
        out_specs=[pl.BlockSpec(memory_space=pltpu.VMEM)] * len(outs),
        scratch_shapes=list(scratch) + [pltpu.SemaphoreType.DMA((fetched,))] * (fetched > 0),
        compiler_params=pltpu.CompilerParams(vmem_limit_bytes=mib * 1024 * 1024),
    )(*[pltpu.with_memory_space_constraint(a, pltpu.HBM) for a in args[:fetched]], *args[fetched:])


def iota(shape, dim):
    return lax.broadcasted_iota(jnp.int32, shape, dim)


def ones_where(mask):
    return jnp.where(mask, 1.0, 0.0).astype(BF16)


def shift_of(size):
    assert size & (size - 1) == 0
    return size.bit_length() - 1


def head_map(rows, cols, row_size, col_size):
    return ones_where(
        (iota((rows, cols), 0) >> shift_of(row_size)) == (iota((rows, cols), 1) >> shift_of(col_size))
    )


def group_reduce(values, size, op):
    lanes = values.shape[1]
    lane = iota(values.shape, 1)
    step = 1
    while step < size:
        partner = jnp.where(
            (lane & step) == 0,
            pltpu.roll(values, lanes - step, 1),
            pltpu.roll(values, step, 1),
        )
        values = op(values, partner)
        step *= 2
    return values


def norm_parts(hidden):
    values = hidden.astype(F32)
    center = values - jnp.mean(values, axis=-1, keepdims=True)
    inverse = lax.rsqrt(jnp.mean(center * center, axis=-1, keepdims=True) + NORM_EPS)
    return center * inverse, inverse


def bit_of(axis, bit):
    return (lax.axis_index(axis) >> shift_of(bit)) & 1


def border_map(border_ref, nodes):
    return ones_where(iota((nodes, border_ref.shape[1]), 0) == border_ref[...])


def fetch(pairs, sems):
    copies = [pltpu.make_async_copy(a, b, sems.at[i]) for i, (a, b) in enumerate(pairs)]
    for copy in copies:
        copy.start()
    return copies


def norm_kernel(
    hidden_hbm, gain_hbm, border_hbm, features_ref, head_ref, tail_ref, hidden_ref, gain_ref, border_ref, sems
):
    pairs = ((hidden_hbm, hidden_ref), (gain_hbm, gain_ref), (border_hbm, border_ref))
    for copy in fetch(pairs, sems):
        copy.wait()
    scaled, _ = norm_parts(hidden_ref[...])
    features = (scaled * gain_ref[...]).astype(BF16)
    features_ref[...] = features
    rows = tn(border_map(border_ref, features.shape[0]), features).astype(BF16)
    rim = head_ref.shape[0]
    head_ref[...] = rows[:rim]
    tail_ref[...] = rows[rim:]


def project_kernel(
    w_hbm, src_hbm, weight_hbm, features_ref, q_ref, kv_ref, mix_ref, w_ref, src_ref, weight_ref, sems
):
    copies = fetch(((src_hbm, src_ref), (weight_hbm, weight_ref), (w_hbm, w_ref)), sems)
    width = features_ref.shape[1]
    rows = iota(mix_ref.shape, 0)
    copies[0].wait()
    copies[1].wait()
    total = jnp.zeros(mix_ref.shape, F32)
    for j in range(src_ref.shape[0]):
        total += jnp.where(rows == src_ref[j : j + 1, :], weight_ref[j : j + 1, :], 0.0)
    mix_ref[...] = total.astype(BF16)
    copies[2].wait()
    qkv = nn(features_ref[...], w_ref[...]).astype(BF16)
    q_ref[...] = qkv[:, :width]
    kv_ref[...] = qkv[:, width:]


def attend_kernel(
    w_out_hbm, bias_hbm, dec_hbm, count_ref, hidden_ref, left_ref, right_ref, q_ref, kv_ref, w_ref,
    src_ref, border_ref, out_ref, projected_ref, head_ref, tail_ref, probs_ref, attended_ref, keys_ref, values_ref, table_ref,
    w_out_ref, bias_ref, dec_ref, sems,
):
    copies = fetch(((bias_hbm, bias_ref), (w_out_hbm, w_out_ref), (dec_hbm, dec_ref)), sems)
    nodes, width = hidden_ref.shape
    rim = left_ref.shape[0]
    edges = src_ref.shape[0]
    columns = bias_ref.shape[1]
    sources = src_ref[...].astype(F32).T
    head_size = width // (columns // edges)
    w_kv = w_ref[:, width:]
    table_ref[:nodes] = kv_ref[...]
    table_ref[nodes : nodes + rim] = nn(left_ref[...], w_kv).astype(BF16)
    table_ref[nodes + rim :] = nn(right_ref[...], w_kv).astype(BF16)
    table = table_ref[...]
    queries = q_ref[...].astype(F32)
    squeeze = head_map(width, columns, head_size, edges)
    expand = head_map(columns, width, edges, head_size)
    lane = iota((nodes, columns), 1) & (edges - 1)
    slot = iota((nodes, table.shape[0]), 1).astype(F32)
    scores = jnp.zeros((nodes, columns), F32)
    for e in range(edges):
        rows = nn(ones_where(slot == sources[:, e : e + 1]), table)
        keys_ref[e] = rows[:, :width].astype(BF16)
        values_ref[e] = rows[:, width:].astype(BF16)
        part = nn((queries * rows[:, :width]).astype(BF16), squeeze)
        scores = jnp.where(lane == e, part, scores)
    copies[0].wait()
    scores = scores / math.sqrt(head_size) + bias_ref[...]
    shifted = jnp.exp(scores - group_reduce(scores, edges, jnp.maximum))
    probs = shifted / group_reduce(shifted, edges, jnp.add)
    probs_ref[...] = probs
    total = jnp.zeros((nodes, width), F32)
    for e in range(edges):
        share = nn(jnp.where(lane == e, probs, 0.0).astype(BF16), expand)
        total += share * values_ref[e].astype(F32)
    attended = total.astype(BF16)
    attended_ref[...] = attended
    copies[1].wait()
    update = hidden_ref[...].astype(F32) + nn(attended, w_out_ref[...])
    live = iota((nodes, width), 0) < count_ref[...]
    node_out = jnp.where(live, update, 0.0).astype(BF16)
    out_ref[...] = node_out
    copies[2].wait()
    projected = nt(dec_ref[...], node_out).astype(BF16)
    projected_ref[...] = projected
    columns = nn(projected, border_map(border_ref, nodes)).astype(BF16)
    head_ref[...] = columns[:, :rim]
    tail_ref[...] = columns[:, rim:]


def join_kernel(left_ref, right_ref, rims_ref):
    rim = left_ref.shape[1]
    rims_ref[:, :rim] = left_ref[...]
    rims_ref[:, rim:] = right_ref[...]


def smooth_root(values):
    return values * values + SMOOTH_SQ


def score_kernel(state_ref, target_ref, area_ref, var_ref, mix_ref, *refs, points):
    grad_ref, head_ref, tail_ref, loss_ref = refs[-4:]
    table_refs = refs[:-4]
    members = len(table_refs) // 2
    fair = 1.0 - (1.0 - ALPHA) / members
    pair = fair / (2.0 * members * (members - 1))
    mix = mix_ref[...]
    nodes = table_refs[0].shape[1]

    def change(n):
        return nn(table_refs[n][...], mix[:nodes]) + nn(table_refs[members + n][...], mix[nodes:])

    own = change(0)
    variables = own.shape[0]
    spread = jnp.zeros_like(own)
    slope = jnp.zeros_like(own)
    for n in range(members):
        gap = own - (change(n) if n else own)
        square = smooth_root(gap)
        inverse = lax.rsqrt(square)
        spread += square * inverse - SMOOTH_ROOT
        slope += gap * inverse
    gap = state_ref[...] + own - target_ref[...]
    square = smooth_root(gap)
    inverse = lax.rsqrt(square)
    square_map = (variables, variables)
    diagonal = iota(square_map, 0) == iota(square_map, 1)
    var = jnp.sum(jnp.where(diagonal, var_ref[...], 0.0), axis=1, keepdims=True)
    weight = area_ref[...] * var / variables
    term = (square * inverse - SMOOTH_ROOT) / members - pair * spread
    loss_ref[...] = jnp.full(loss_ref.shape, jnp.sum(term * weight) / points, F32)
    grad = ((gap * inverse / members - 2.0 * pair * slope) * weight).astype(BF16)
    grad_ref[...] = grad
    rim = head_ref.shape[1]
    nodes = mix_ref.shape[0] - 2 * rim
    columns = nt(grad, mix_ref[nodes:, :]).astype(BF16)
    head_ref[...] = columns[:, :rim]
    tail_ref[...] = columns[:, rim:]


def own_rows_kernel(mix_ref, grad_ref, src_ref, own_ref, hot_ref):
    nodes = own_ref.shape[1]
    own_ref[...] = nt(grad_ref[...], mix_ref[:nodes, :])
    slot = iota((hot_ref.shape[0], nodes), 0)
    for e in range(src_ref.shape[0]):
        hot_ref[:, e * nodes : (e + 1) * nodes] = ones_where(slot == src_ref[e : e + 1, :])


def padded(variables):
    return -(-variables // 8) * 8


def split_halves(mine, source_ref, send_ref, keep_ref):
    for i in range(send_ref.shape[0]):
        send_ref[i] = source_ref[i, 1 - mine].astype(BF16)
        keep_ref[i] = source_ref[i, mine]


def put(full_ref, start, values):
    shape = full_ref.shape[:3]
    full_ref[:, :, :, start : start + values.shape[1]] = values.reshape(*shape, values.shape[1])


def value_back_kernel(
    count_ref, own_ref, from_left_ref, from_right_ref, border_ref, node_out_ref, w_dec_ref,
    attended_ref, w_out_ref, probs_ref, hot_ref, features_ref, left_ref, right_ref, loss_ref,
    grad_ref, mixed_ref, grad_value_ref, send_ref, keep_ref, edge_ref, full_ref,
):
    nodes, width = grad_ref.shape
    rim = left_ref.shape[0]
    columns = probs_ref.shape[1]
    edges = hot_ref.shape[1] // nodes
    head_size = width // (columns // edges)
    returned = jnp.concatenate([from_left_ref[...], from_right_ref[...]], axis=1)
    columns_grad = own_ref[...] + nt(returned, border_map(border_ref, nodes))
    live = iota(columns_grad.shape, 1) < count_ref[...]
    columns_grad = jnp.where(live, columns_grad, 0.0).astype(BF16)
    total = tn(columns_grad, w_dec_ref[...])
    grad_ref[...] = total
    rounded = total.astype(BF16)
    mixed = nt(rounded, w_out_ref[...]).astype(BF16)
    mixed_ref[...] = mixed
    mixed = mixed.astype(F32)
    expand = head_map(columns, width, edges, head_size)
    lane = iota((nodes, columns), 1) & (edges - 1)
    probs = probs_ref[...]
    for e in range(edges):
        share = nn(jnp.where(lane == e, probs, 0.0).astype(BF16), expand)
        edge_ref[e * nodes : (e + 1) * nodes, :] = (share * mixed).astype(BF16)
    grad_value = nn(hot_ref[...], edge_ref[...]).astype(BF16)
    grad_value_ref[...] = grad_value
    features = features_ref[...]
    total = tn(features, grad_value[:nodes])
    total += tn(left_ref[...], grad_value[nodes : nodes + rim])
    total += tn(right_ref[...], grad_value[nodes + rim :])
    put(full_ref, 0, total)
    variables = columns_grad.shape[0]
    step = padded(variables)
    columns_grad = jnp.concatenate(
        [columns_grad.astype(F32), jnp.zeros((step - variables, nodes), F32)], axis=0
    ).astype(BF16)
    loss = jnp.broadcast_to(loss_ref[0:1, 0:1], (2 * LANES - 2 * step, width))
    high = loss.astype(BF16).astype(F32)
    row = iota(loss.shape, 0)
    loss = jnp.where(row == 0, high, jnp.where(row == 1, loss - high, 0.0))
    few = [nn(columns_grad, attended_ref[...]), nn(columns_grad, node_out_ref[...]), loss]
    put(full_ref, width, jnp.concatenate(few, axis=0).T)
    split_halves(bit_of("member", 1), full_ref, send_ref, keep_ref)


def score_back_kernel(mixed_ref, probs_ref, values_ref, q_ref, keys_ref, grad_query_ref, edge_ref):
    nodes, width = mixed_ref.shape
    edges = values_ref.shape[0]
    columns = probs_ref.shape[1]
    head_size = width // (columns // edges)
    inv_root = 1.0 / math.sqrt(head_size)
    squeeze = head_map(width, columns, head_size, edges)
    expand = head_map(columns, width, edges, head_size)
    lane = iota((nodes, columns), 1) & (edges - 1)
    mixed = mixed_ref[...].astype(F32)
    probs = probs_ref[...]
    grad_probs = jnp.zeros((nodes, columns), F32)
    for e in range(edges):
        part = nn((mixed * values_ref[e].astype(F32)).astype(BF16), squeeze)
        grad_probs = jnp.where(lane == e, part, grad_probs)
    grad_scores = probs * (grad_probs - group_reduce(probs * grad_probs, edges, jnp.add))
    query = q_ref[...].astype(F32) * inv_root
    total = jnp.zeros((nodes, width), F32)
    for e in range(edges):
        share = nn(jnp.where(lane == e, grad_scores, 0.0).astype(BF16), expand)
        total += share * keys_ref[e].astype(F32)
        edge_ref[e * nodes : (e + 1) * nodes, :] = (share * query).astype(BF16)
    grad_query_ref[...] = (total * inv_root).astype(BF16)


def query_back_kernel(edge_ref, hot_ref, grad_value_ref, w_ref, grad_key_ref, head_ref, tail_ref):
    width = edge_ref.shape[1]
    rim = head_ref.shape[0]
    nodes = hot_ref.shape[0] - 2 * rim
    grad_key = nn(hot_ref[...], edge_ref[...]).astype(BF16)
    grad_key_ref[...] = grad_key
    rows = nt(grad_key[nodes:], w_ref[:, width : 2 * width])
    rows += nt(grad_value_ref[nodes:, :], w_ref[:, 2 * width :])
    rows = rows.astype(BF16)
    head_ref[...] = rows[:rim]
    tail_ref[...] = rows[rim:]


def query_weight_kernel(
    features_ref, left_ref, right_ref, grad_query_ref, grad_key_ref, send_ref, keep_ref, full_ref
):
    nodes, width = features_ref.shape
    rim = left_ref.shape[0]
    features = features_ref[...]
    put(full_ref, 0, tn(features, grad_query_ref[...]))
    total = tn(features, grad_key_ref[:nodes, :])
    total += tn(left_ref[...], grad_key_ref[nodes : nodes + rim, :])
    total += tn(right_ref[...], grad_key_ref[nodes + rim :, :])
    put(full_ref, width, total)
    split_halves(bit_of("member", 1), full_ref, send_ref, keep_ref)


def joined(keep, arrived, variables):
    total = keep + arrived.astype(F32)
    if variables is None:
        return total
    last = total[..., -LANES:]
    lane = iota(last.shape, last.ndim - 1)
    at = 2 * padded(variables) - LANES
    loss = last[..., at : at + 1] + last[..., at + 1 : at + 2]
    high = loss.astype(BF16).astype(F32)
    last = jnp.where(lane == at, high, last)
    last = jnp.where(lane == at + 1, loss - high, last)
    return jnp.concatenate([total[..., :-LANES], last], axis=-1)


def combine_kernel(keep_in_ref, arrived_ref, send_ref, keep_ref, *, axis, bit, variables):
    mine = bit_of(axis, bit)
    for i in range(send_ref.shape[0]):
        away = 1 - mine
        send_ref[i] = joined(keep_in_ref[i, away], arrived_ref[i, away], variables).astype(BF16)
        keep_ref[i] = joined(keep_in_ref[i, mine], arrived_ref[i, mine], variables)


def merge_kernel(
    query_keep_ref, query_in_ref, value_keep_ref, value_in_ref, send_ref, keep_ref, *, axis, bit, variables
):
    mine = bit_of(axis, bit)
    start = query_keep_ref.shape[-1]
    for at, out_ref in ((1 - mine, send_ref), (mine, keep_ref)):
        for i in range(send_ref.shape[0]):
            query = joined(query_keep_ref[i, at], query_in_ref[i, at], None)
            value = joined(value_keep_ref[i, at], value_in_ref[i, at], variables)
            out_ref[i, :, :start] = query.astype(out_ref.dtype)
            out_ref[i, :, start:] = value.astype(out_ref.dtype)


def total_kernel(keep_ref, arrived_ref, sum_ref, *, variables):
    for i in range(sum_ref.shape[0]):
        sum_ref[i] = joined(keep_ref[i], arrived_ref[i], variables).astype(BF16)


def swapped(array, axis, bit):
    count = lax.axis_size(axis)
    return lax.ppermute(array, axis, [(i, i ^ bit) for i in range(count)])


def from_members(array, members):
    others = {away: swapped(array, "member", away) for away in reversed(range(1, members))}
    return [array] + [others[away] for away in range(1, members)]


class Halving:
    def __init__(self, regions, members, rows):
        self.left = [("region", 1 << b) for b in reversed(range(shift_of(regions)))]
        self.left += [("member", 1 << b) for b in reversed(range(shift_of(members)))]
        self.rows = rows

    def half(self, step, packed):
        place = self.left.index(step)
        half = (1 << place, (1 << (len(self.left) - 1 - place)) * self.rows, packed)
        return half, (half[0], 2) + half[1:]

    def run(self, send, keep, steps, variables):
        packed = send.shape[-1]
        for i, (axis, bit) in enumerate(steps):
            arrived = swapped(send, axis, bit)
            self.left.remove((axis, bit))
            if i + 1 == len(steps):
                return keep, arrived
            half, both = self.half(steps[i + 1], packed)
            send, keep = on_core(
                functools.partial(
                    combine_kernel, axis=steps[i + 1][0], bit=steps[i + 1][1], variables=variables
                ),
                [(half, BF16), (half, F32)],
                keep.reshape(both), arrived.reshape(both),
            )


def unpack_kernel(w_dec_ref, *refs):
    sum_refs = refs[:-4]
    qkv_ref, out_ref, dec_ref, loss_ref = refs[-4:]
    width = out_ref.shape[-1]
    variables = dec_ref.shape[-1]
    step = padded(variables)
    start = 3 * width
    place = lax.axis_index("member")
    for away, ref in enumerate(sum_refs):
        at = place ^ away
        qkv_ref[at] = ref[:, :start].astype(F32)
        out_ref[at] = nn(ref[:, start : start + variables], w_dec_ref[...])
        dec_ref[at] = ref[:, start + step : start + step + variables].astype(F32)
    start += 2 * step
    last = sum_refs[0][0:1, start : start + 2].astype(F32)
    loss_ref[...] = last[:, 0:1] + last[:, 1:2]


def own_feature_kernel(grad_query_ref, grad_key_ref, grad_value_ref, w_ref, grad_ref):
    nodes, width = grad_query_ref.shape
    total = nt(grad_query_ref[...], w_ref[:, :width])
    total += nt(grad_key_ref[:nodes, :], w_ref[:, width : 2 * width])
    grad_ref[...] = total + nt(grad_value_ref[:nodes, :], w_ref[:, 2 * width :])


def latent_grad_kernel(
    hidden_ref, gain_ref, own_ref, from_left_ref, from_right_ref, border_ref, node_ref, grad_ref, rows_ref
):
    nodes = hidden_ref.shape[0]
    rim = from_left_ref.shape[0]
    rows_ref[:rim] = from_left_ref[...]
    rows_ref[rim:] = from_right_ref[...]
    mask = ones_where(iota((nodes, 2 * rim), 0) == border_ref[...])
    grad_rows = own_ref[...] + nn(mask, rows_ref[...])
    scaled, inverse = norm_parts(hidden_ref[...])
    scaled_grad = grad_rows * gain_ref[...]
    back = inverse * (
        scaled_grad
        - jnp.mean(scaled_grad, axis=-1, keepdims=True)
        - scaled * jnp.mean(scaled_grad * scaled, axis=-1, keepdims=True)
    )
    grad_ref[...] = (node_ref[...] + back).astype(BF16)


def swap_rims(head, tail):
    count = lax.axis_size("region")
    from_left = lax.ppermute(tail, "region", [(i, (i + 1) % count) for i in range(count)])
    from_right = lax.ppermute(head, "region", [((i + 1) % count, i) for i in range(count)])
    return from_left, from_right


def layer(
    latent,
    node_gain,
    w_qkv,
    w_out,
    edge_bias,
    edge_source,
    boundary,
    node_count,
    decoder_projection_weight,
    dec_source,
    dec_weight,
    state,
    target,
    area,
    var_weight,
):
    hidden = latent[0]
    nodes, width = hidden.shape
    rim = boundary.shape[1] // 2
    table_rows = nodes + 2 * rim
    sources = edge_source.T
    edges = sources.shape[0]
    w_decoder = decoder_projection_weight.T
    count = node_count[None]
    columns = edge_bias.shape[1]
    variables, points = state.shape
    regions, members = lax.axis_size("region"), lax.axis_size("member")
    total_points = points * regions
    gain = node_gain[None]
    rim_rows = ((rim, width), BF16)
    rim_columns = ((variables, rim), BF16)
    features, head, tail = on_core(
        norm_kernel,
        [((nodes, width), BF16), rim_rows, rim_rows],
        hidden, gain, boundary,
        fetched=3,
        scratch=[
            pltpu.VMEM((nodes, width), BF16), pltpu.VMEM((1, width), F32), pltpu.VMEM((1, 2 * rim), jnp.int32),
        ],
        mib=4,
    )
    left, right = swap_rims(head, tail)
    queries, own_kv, mix, w_qkv = on_core(
        project_kernel,
        [
            ((nodes, width), BF16), ((nodes, 2 * width), BF16), ((table_rows, points), BF16),
            ((width, 3 * width), BF16),
        ],
        w_qkv, dec_source, dec_weight, features,
        fetched=3,
        scratch=[pltpu.VMEM(dec_source.shape, jnp.int32), pltpu.VMEM(dec_weight.shape, F32)],
    )
    edge_rows = ((edges, nodes, width), BF16)
    node_out, projected, head, tail, probs, attended, keys, values = on_core(
        attend_kernel,
        [
            ((nodes, width), BF16), ((variables, nodes), BF16), rim_columns, rim_columns,
            ((nodes, columns), F32), ((nodes, width), BF16), edge_rows, edge_rows,
        ],
        w_out, edge_bias, w_decoder, count, hidden, left, right, queries, own_kv, w_qkv, sources, boundary,
        fetched=3,
        scratch=[
            pltpu.VMEM((table_rows, 2 * width), BF16), pltpu.VMEM((width, width), BF16),
            pltpu.VMEM((nodes, columns), F32), pltpu.VMEM((variables, width), BF16),
        ],
        mib=16,
    )
    out_left, out_right = swap_rims(head, tail)
    core = [("member", 1)]
    across = [("member", 1 << b) for b in range(1, shift_of(members))]
    own_tables = from_members(projected, members)
    (rims,) = on_core(join_kernel, [((variables, 2 * rim), BF16)], out_left, out_right)
    rim_tables = from_members(rims, members)
    grad, head, tail, loss = on_core(
        functools.partial(score_kernel, points=total_points),
        [((variables, points), BF16), rim_columns, rim_columns, ((1, LANES), F32)],
        state, target, area[None], var_weight[None], mix, *own_tables, *rim_tables,
    )
    back_left, back_right = swap_rims(head, tail)
    grad_own, hot = on_core(
        own_rows_kernel,
        [((variables, nodes), F32), ((table_rows, edges * nodes), BF16)],
        mix, grad, sources,
    )
    rows = width // (regions * members)
    pieces = regions * members // 2

    def halves(packed):
        return [((pieces, rows, packed), BF16), ((pieces, rows, packed), F32)]

    def whole(packed):
        return pltpu.VMEM((pieces, 2, rows, packed), F32)

    grad_node, grad_mixed, grad_value, value_send, value_keep = on_core(
        value_back_kernel,
        [((nodes, width), F32), ((nodes, width), BF16), ((table_rows, width), BF16)]
        + halves(width + 2 * LANES),
        count, grad_own, back_left, back_right, boundary, node_out, w_decoder,
        attended, w_out, probs, hot, features, left, right, loss,
        scratch=[pltpu.VMEM((edges * nodes, width), BF16), whole(width + 2 * LANES)],
        mib=16,
    )
    grad_query, key_edges = on_core(
        score_back_kernel,
        [((nodes, width), BF16), ((edges * nodes, width), BF16)],
        grad_mixed, probs, values, queries, keys,
    )
    grad_key, head, tail = on_core(
        query_back_kernel,
        [((table_rows, width), BF16), rim_rows, rim_rows],
        key_edges, hot, grad_value, w_qkv,
    )
    rim_left, rim_right = swap_rims(head, tail)
    query_send, query_keep = on_core(
        query_weight_kernel,
        halves(2 * width),
        features, left, right, grad_query, grad_key,
        scratch=[whole(2 * width)],
    )
    (own_feature,) = on_core(own_feature_kernel, [((nodes, width), F32)], grad_query, grad_key, grad_value, w_qkv)
    (grad_latent,) = on_core(
        latent_grad_kernel,
        [((nodes, width), BF16)],
        hidden, gain, own_feature, rim_left, rim_right, boundary, grad_node,
        scratch=[pltpu.VMEM((2 * rim, width), BF16)],
    )

    around = [("region", 1 << b) for b in range(shift_of(regions))]
    around[:2] = around[1::-1]
    value_sum, query_sum = Halving(regions, members, rows), Halving(regions, members, rows)
    value_keep, value_in = value_sum.run(value_send, value_keep, core + across + around[:1], variables)
    query_keep, query_in = query_sum.run(query_send, query_keep, core + across + around[:1], None)
    packed = 3 * width + 2 * LANES
    half, _ = value_sum.half(around[1], packed)
    _, both_values = value_sum.half(around[1], width + 2 * LANES)
    _, both_queries = value_sum.half(around[1], 2 * width)
    send, keep = on_core(
        functools.partial(merge_kernel, axis=around[1][0], bit=around[1][1], variables=variables),
        [(half, BF16), (half, F32)],
        query_keep.reshape(both_queries), query_in.reshape(both_queries),
        value_keep.reshape(both_values), value_in.reshape(both_values),
    )
    keep, arrived = value_sum.run(send, keep, around[1:], variables)
    piece = (1, rows, packed)
    (total,) = on_core(
        functools.partial(total_kernel, variables=variables), [(piece, BF16)],
        keep.reshape(piece), arrived.reshape(piece),
    )
    sums = from_members(total.reshape(rows, packed), members)
    share_qkv, share_out, share_dec, loss = on_core(
        unpack_kernel,
        [
            ((members, rows, 3 * width), F32), ((members, rows, width), F32),
            ((members, rows, variables), F32), ((1, 1), F32),
        ],
        w_decoder, *sums,
    )
    held = members * rows
    return (
        loss.reshape(()),
        share_qkv.reshape(held, 3 * width),
        share_out.reshape(held, width),
        share_dec.reshape(held, variables),
        grad_latent[None],
    )


def solution(mesh):
    placed = (
        P("member", "region", None),
        P(),
        P(),
        P(),
        P("region", None),
        P("region", None),
        P("region", None),
        P("region"),
        P(),
        P(None, "region"),
        P(None, "region"),
        P(None, "region"),
        P(None, "region"),
        P("region"),
        P(),
    )
    return jax.shard_map(
        layer,
        mesh=mesh,
        in_specs=placed,
        out_specs=(
            P(),
            P("region", None),
            P("region", None),
            P("region", None),
            P("member", "region", None),
        ),
        check_vma=False,
    )
```

```python
import functools
import math

import jax
import jax.numpy as jnp
from jax import lax
from jax.experimental import pallas as pl
from jax.experimental.pallas import tpu as pltpu
from jax.sharding import PartitionSpec as P


ALPHA = 0.95
NORM_EPS = 1e-05
SMOOTH_SQ = 0.25
SMOOTH_ROOT = 0.5
F32 = jnp.float32
BF16 = jnp.bfloat16
LANES = 128


def nn(left, right):
    return lax.dot_general(left, right, (((1,), (0,)), ((), ())), preferred_element_type=F32)


def nt(left, right):
    return lax.dot_general(left, right, (((1,), (1,)), ((), ())), preferred_element_type=F32)


def tn(left, right):
    return lax.dot_general(left, right, (((0,), (0,)), ((), ())), preferred_element_type=F32)


def on_core(kernel, outs, *args, fetched=0, scratch=(), mib=8):
    return pl.pallas_call(
        kernel,
        out_shape=[jax.ShapeDtypeStruct(s, d) for s, d in outs],
        in_specs=[pl.BlockSpec(memory_space=pltpu.HBM)] * fetched
        + [pl.BlockSpec(memory_space=pltpu.VMEM)] * (len(args) - fetched),
        out_specs=[pl.BlockSpec(memory_space=pltpu.VMEM)] * len(outs),
        scratch_shapes=list(scratch) + [pltpu.SemaphoreType.DMA((fetched,))] * (fetched > 0),
        compiler_params=pltpu.CompilerParams(vmem_limit_bytes=mib * 1024 * 1024),
    )(*[pltpu.with_memory_space_constraint(a, pltpu.HBM) for a in args[:fetched]], *args[fetched:])


def iota(shape, dim):
    return lax.broadcasted_iota(jnp.int32, shape, dim)


def ones_where(mask):
    return jnp.where(mask, 1.0, 0.0).astype(BF16)


def shift_of(size):
    assert size & (size - 1) == 0
    return size.bit_length() - 1


def head_map(rows, cols, row_size, col_size):
    return ones_where(
        (iota((rows, cols), 0) >> shift_of(row_size)) == (iota((rows, cols), 1) >> shift_of(col_size))
    )


def group_reduce(values, size, op):
    lanes = values.shape[1]
    lane = iota(values.shape, 1)
    step = 1
    while step < size:
        partner = jnp.where(
            (lane & step) == 0,
            pltpu.roll(values, lanes - step, 1),
            pltpu.roll(values, step, 1),
        )
        values = op(values, partner)
        step *= 2
    return values


def norm_parts(hidden):
    values = hidden.astype(F32)
    center = values - jnp.mean(values, axis=-1, keepdims=True)
    inverse = lax.rsqrt(jnp.mean(center * center, axis=-1, keepdims=True) + NORM_EPS)
    return center * inverse, inverse


def bit_of(axis, bit):
    return (lax.axis_index(axis) >> shift_of(bit)) & 1


def border_map(border_ref, nodes):
    return ones_where(iota((nodes, border_ref.shape[1]), 0) == border_ref[...])


def fetch(pairs, sems):
    copies = [pltpu.make_async_copy(a, b, sems.at[i]) for i, (a, b) in enumerate(pairs)]
    for copy in copies:
        copy.start()
    return copies


def norm_kernel(
    hidden_hbm, gain_hbm, border_hbm, features_ref, head_ref, tail_ref, hidden_ref, gain_ref, border_ref, sems
):
    pairs = ((hidden_hbm, hidden_ref), (gain_hbm, gain_ref), (border_hbm, border_ref))
    for copy in fetch(pairs, sems):
        copy.wait()
    scaled, _ = norm_parts(hidden_ref[...])
    features = (scaled * gain_ref[...]).astype(BF16)
    features_ref[...] = features
    rows = tn(border_map(border_ref, features.shape[0]), features).astype(BF16)
    rim = head_ref.shape[0]
    head_ref[...] = rows[:rim]
    tail_ref[...] = rows[rim:]


def project_kernel(
    w_hbm, src_hbm, weight_hbm, edge_hbm, features_ref, q_ref, own_ref, mix_ref, w_ref,
    src_ref, weight_ref, edge_ref, sems,
):
    pairs = ((src_hbm, src_ref), (weight_hbm, weight_ref), (w_hbm, w_ref), (edge_hbm, edge_ref))
    copies = fetch(pairs, sems)
    width = features_ref.shape[1]
    rows = iota(mix_ref.shape, 0)
    copies[0].wait()
    copies[1].wait()
    total = jnp.zeros(mix_ref.shape, F32)
    for j in range(src_ref.shape[0]):
        total += jnp.where(rows == src_ref[j : j + 1, :], weight_ref[j : j + 1, :], 0.0)
    mix_ref[...] = total.astype(BF16)
    copies[2].wait()
    qkv = nn(features_ref[...], w_ref[...]).astype(BF16)
    q_ref[...] = qkv[:, :width]
    key_value = qkv[:, width:]
    copies[3].wait()
    nodes = features_ref.shape[0]
    sources = edge_ref[...].astype(F32).T
    slot = iota((nodes, nodes), 1).astype(F32)
    for e in range(own_ref.shape[0]):
        own_ref[e] = nn(ones_where(slot == sources[:, e : e + 1]), key_value).astype(BF16)


def attend_kernel(
    w_out_hbm, bias_hbm, dec_hbm, count_ref, hidden_ref, left_ref, right_ref, q_ref, own_ref, w_ref,
    src_ref, border_ref, out_ref, projected_ref, head_ref, tail_ref, probs_ref, attended_ref, keys_ref, values_ref, shares_ref, table_ref,
    w_out_ref, bias_ref, dec_ref, sems,
):
    copies = fetch(((bias_hbm, bias_ref), (w_out_hbm, w_out_ref), (dec_hbm, dec_ref)), sems)
    nodes, width = hidden_ref.shape
    rim = left_ref.shape[0]
    edges = src_ref.shape[0]
    columns = bias_ref.shape[1]
    sources = src_ref[...].astype(F32).T
    head_size = width // (columns // edges)
    w_kv = w_ref[:, width:]
    table_ref[:rim] = nn(left_ref[...], w_kv).astype(BF16)
    table_ref[rim:] = nn(right_ref[...], w_kv).astype(BF16)
    table = table_ref[...]
    queries = q_ref[...].astype(F32)
    squeeze = head_map(width, columns, head_size, edges)
    expand = head_map(columns, width, edges, head_size)
    lane = iota((nodes, columns), 1) & (edges - 1)
    slot = (iota((nodes, table.shape[0]), 1) + nodes).astype(F32)
    scores = jnp.zeros((nodes, columns), F32)
    for e in range(edges):
        rows = nn(ones_where(slot == sources[:, e : e + 1]), table) + own_ref[e].astype(F32)
        keys_ref[e] = rows[:, :width].astype(BF16)
        values_ref[e] = rows[:, width:].astype(BF16)
        part = nn((queries * rows[:, :width]).astype(BF16), squeeze)
        scores = jnp.where(lane == e, part, scores)
    copies[0].wait()
    scores = scores / math.sqrt(head_size) + bias_ref[...]
    shifted = jnp.exp(scores - group_reduce(scores, edges, jnp.maximum))
    probs = shifted / group_reduce(shifted, edges, jnp.add)
    probs_ref[...] = probs
    total = jnp.zeros((nodes, width), F32)
    for e in range(edges):
        share = nn(jnp.where(lane == e, probs, 0.0).astype(BF16), expand)
        shares_ref[e] = share.astype(BF16)
        total += share * values_ref[e].astype(F32)
    attended = total.astype(BF16)
    attended_ref[...] = attended
    copies[1].wait()
    update = hidden_ref[...].astype(F32) + nn(attended, w_out_ref[...])
    live = iota((nodes, width), 0) < count_ref[...]
    node_out = jnp.where(live, update, 0.0).astype(BF16)
    out_ref[...] = node_out
    copies[2].wait()
    projected = nt(dec_ref[...], node_out).astype(BF16)
    projected_ref[...] = projected
    columns = nn(projected, border_map(border_ref, nodes)).astype(BF16)
    head_ref[...] = columns[:, :rim]
    tail_ref[...] = columns[:, rim:]


def join_kernel(left_ref, right_ref, rims_ref):
    rim = left_ref.shape[1]
    rims_ref[:, :rim] = left_ref[...]
    rims_ref[:, rim:] = right_ref[...]


def smooth_root(values):
    return values * values + SMOOTH_SQ


def score_kernel(state_ref, target_ref, area_ref, var_ref, mix_ref, *refs, points):
    grad_ref, head_ref, tail_ref, loss_ref = refs[-4:]
    table_refs = refs[:-4]
    members = len(table_refs) // 2
    fair = 1.0 - (1.0 - ALPHA) / members
    pair = fair / (2.0 * members * (members - 1))
    mix = mix_ref[...]
    nodes = table_refs[0].shape[1]

    def change(n):
        return nn(table_refs[n][...], mix[:nodes]) + nn(table_refs[members + n][...], mix[nodes:])

    own = change(0)
    variables = own.shape[0]
    spread = jnp.zeros_like(own)
    slope = jnp.zeros_like(own)
    for n in range(members):
        gap = own - (change(n) if n else own)
        square = smooth_root(gap)
        inverse = lax.rsqrt(square)
        spread += square * inverse - SMOOTH_ROOT
        slope += gap * inverse
    gap = state_ref[...] + own - target_ref[...]
    square = smooth_root(gap)
    inverse = lax.rsqrt(square)
    square_map = (variables, variables)
    diagonal = iota(square_map, 0) == iota(square_map, 1)
    var = jnp.sum(jnp.where(diagonal, var_ref[...], 0.0), axis=1, keepdims=True)
    weight = area_ref[...] * var / variables
    term = (square * inverse - SMOOTH_ROOT) / members - pair * spread
    loss_ref[...] = jnp.full(loss_ref.shape, jnp.sum(term * weight) / points, F32)
    grad = ((gap * inverse / members - 2.0 * pair * slope) * weight).astype(BF16)
    grad_ref[...] = grad
    rim = head_ref.shape[1]
    nodes = mix_ref.shape[0] - 2 * rim
    columns = nt(grad, mix_ref[nodes:, :]).astype(BF16)
    head_ref[...] = columns[:, :rim]
    tail_ref[...] = columns[:, rim:]


def own_rows_kernel(mix_ref, grad_ref, src_ref, own_ref, hot_ref):
    nodes = own_ref.shape[1]
    own_ref[...] = nt(grad_ref[...], mix_ref[:nodes, :])
    slot = iota((hot_ref.shape[0], nodes), 0)
    for e in range(src_ref.shape[0]):
        hot_ref[:, e * nodes : (e + 1) * nodes] = ones_where(slot == src_ref[e : e + 1, :])


def padded(variables):
    return -(-variables // 8) * 8


def split_halves(mine, source_ref, send_ref, keep_ref):
    for i in range(send_ref.shape[0]):
        send_ref[i] = source_ref[i, 1 - mine].astype(BF16)
        keep_ref[i] = source_ref[i, mine]


def put(full_ref, start, values):
    shape = full_ref.shape[:3]
    full_ref[:, :, :, start : start + values.shape[1]] = values.reshape(*shape, values.shape[1])


def value_back_kernel(
    count_ref, own_ref, from_left_ref, from_right_ref, border_ref, node_out_ref, w_dec_ref,
    attended_ref, w_out_ref, shares_ref, hot_ref, features_ref, left_ref, right_ref, loss_ref,
    grad_ref, mixed_ref, grad_value_ref, send_ref, keep_ref, edge_ref, full_ref,
):
    nodes, width = grad_ref.shape
    rim = left_ref.shape[0]
    edges = shares_ref.shape[0]
    returned = jnp.concatenate([from_left_ref[...], from_right_ref[...]], axis=1)
    columns_grad = own_ref[...] + nt(returned, border_map(border_ref, nodes))
    live = iota(columns_grad.shape, 1) < count_ref[...]
    columns_grad = jnp.where(live, columns_grad, 0.0).astype(BF16)
    total = tn(columns_grad, w_dec_ref[...])
    grad_ref[...] = total
    rounded = total.astype(BF16)
    mixed = nt(rounded, w_out_ref[...]).astype(BF16)
    mixed_ref[...] = mixed
    mixed = mixed.astype(F32)
    for e in range(edges):
        edge_ref[e * nodes : (e + 1) * nodes, :] = (shares_ref[e].astype(F32) * mixed).astype(BF16)
    grad_value = nn(hot_ref[...], edge_ref[...]).astype(BF16)
    grad_value_ref[...] = grad_value
    features = features_ref[...]
    total = tn(features, grad_value[:nodes])
    total += tn(left_ref[...], grad_value[nodes : nodes + rim])
    total += tn(right_ref[...], grad_value[nodes + rim :])
    put(full_ref, 0, total)
    variables = columns_grad.shape[0]
    step = padded(variables)
    columns_grad = jnp.concatenate(
        [columns_grad.astype(F32), jnp.zeros((step - variables, nodes), F32)], axis=0
    ).astype(BF16)
    loss = jnp.broadcast_to(loss_ref[0:1, 0:1], (2 * LANES - 2 * step, width))
    high = loss.astype(BF16).astype(F32)
    row = iota(loss.shape, 0)
    loss = jnp.where(row == 0, high, jnp.where(row == 1, loss - high, 0.0))
    few = [nn(columns_grad, attended_ref[...]), nn(columns_grad, node_out_ref[...]), loss]
    put(full_ref, width, jnp.concatenate(few, axis=0).T)
    split_halves(bit_of("member", 1), full_ref, send_ref, keep_ref)


def score_back_kernel(mixed_ref, probs_ref, values_ref, q_ref, keys_ref, grad_query_ref, edge_ref):
    nodes, width = mixed_ref.shape
    edges = values_ref.shape[0]
    columns = probs_ref.shape[1]
    head_size = width // (columns // edges)
    inv_root = 1.0 / math.sqrt(head_size)
    squeeze = head_map(width, columns, head_size, edges)
    expand = head_map(columns, width, edges, head_size)
    lane = iota((nodes, columns), 1) & (edges - 1)
    mixed = mixed_ref[...].astype(F32)
    probs = probs_ref[...]
    grad_probs = jnp.zeros((nodes, columns), F32)
    for e in range(edges):
        part = nn((mixed * values_ref[e].astype(F32)).astype(BF16), squeeze)
        grad_probs = jnp.where(lane == e, part, grad_probs)
    grad_scores = probs * (grad_probs - group_reduce(probs * grad_probs, edges, jnp.add))
    query = q_ref[...].astype(F32) * inv_root
    total = jnp.zeros((nodes, width), F32)
    for e in range(edges):
        share = nn(jnp.where(lane == e, grad_scores, 0.0).astype(BF16), expand)
        total += share * keys_ref[e].astype(F32)
        edge_ref[e * nodes : (e + 1) * nodes, :] = (share * query).astype(BF16)
    grad_query_ref[...] = (total * inv_root).astype(BF16)


def query_back_kernel(edge_ref, hot_ref, grad_value_ref, w_ref, grad_key_ref, head_ref, tail_ref):
    width = edge_ref.shape[1]
    rim = head_ref.shape[0]
    nodes = hot_ref.shape[0] - 2 * rim
    grad_key = nn(hot_ref[...], edge_ref[...]).astype(BF16)
    grad_key_ref[...] = grad_key
    rows = nt(grad_key[nodes:], w_ref[:, width : 2 * width])
    rows += nt(grad_value_ref[nodes:, :], w_ref[:, 2 * width :])
    rows = rows.astype(BF16)
    head_ref[...] = rows[:rim]
    tail_ref[...] = rows[rim:]


def query_weight_kernel(
    features_ref, left_ref, right_ref, grad_query_ref, grad_key_ref, send_ref, keep_ref, full_ref
):
    nodes, width = features_ref.shape
    rim = left_ref.shape[0]
    features = features_ref[...]
    put(full_ref, 0, tn(features, grad_query_ref[...]))
    total = tn(features, grad_key_ref[:nodes, :])
    total += tn(left_ref[...], grad_key_ref[nodes : nodes + rim, :])
    total += tn(right_ref[...], grad_key_ref[nodes + rim :, :])
    put(full_ref, width, total)
    split_halves(bit_of("member", 1), full_ref, send_ref, keep_ref)


def joined(keep, arrived, variables):
    total = keep + arrived.astype(F32)
    if variables is None:
        return total
    last = total[..., -LANES:]
    lane = iota(last.shape, last.ndim - 1)
    at = 2 * padded(variables) - LANES
    loss = last[..., at : at + 1] + last[..., at + 1 : at + 2]
    high = loss.astype(BF16).astype(F32)
    last = jnp.where(lane == at, high, last)
    last = jnp.where(lane == at + 1, loss - high, last)
    return jnp.concatenate([total[..., :-LANES], last], axis=-1)


def combine_kernel(keep_in_ref, arrived_ref, send_ref, keep_ref, *, axis, bit, variables):
    mine = bit_of(axis, bit)
    for i in range(send_ref.shape[0]):
        away = 1 - mine
        send_ref[i] = joined(keep_in_ref[i, away], arrived_ref[i, away], variables).astype(BF16)
        keep_ref[i] = joined(keep_in_ref[i, mine], arrived_ref[i, mine], variables)


def part_kernel(
    keep_a_ref, in_a_ref, keep_b_ref, in_b_ref,
    query_send_ref, query_keep_ref, key_send_ref, key_keep_ref, *, steps,
):
    width = query_send_ref.shape[-1]
    cases = (
        (steps[0], keep_a_ref, in_a_ref, query_send_ref, query_keep_ref, slice(0, width)),
        (steps[1], keep_b_ref, in_b_ref, key_send_ref, key_keep_ref, slice(width, 2 * width)),
    )
    for (axis, bit), keep_in_ref, in_ref, send_ref, keep_ref, columns in cases:
        mine = bit_of(axis, bit)
        for at, out_ref in ((1 - mine, send_ref), (mine, keep_ref)):
            for i in range(send_ref.shape[0]):
                total = joined(keep_in_ref[i, at, :, columns], in_ref[i, at, :, columns], None)
                out_ref[i] = total.astype(out_ref.dtype)


def merge_kernel(*refs, axis, bit, variables):
    send_ref, keep_ref = refs[-2:]
    chains = [refs[i : i + 2] for i in range(0, len(refs) - 2, 2)]
    mine = bit_of(axis, bit)
    for at, out_ref in ((1 - mine, send_ref), (mine, keep_ref)):
        for i in range(send_ref.shape[0]):
            start = 0
            for n, (keep_in_ref, in_ref) in enumerate(chains):
                total = joined(
                    keep_in_ref[i, at], in_ref[i, at], variables if n + 1 == len(chains) else None
                )
                out_ref[i, :, start : start + total.shape[-1]] = total.astype(out_ref.dtype)
                start += total.shape[-1]


def total_kernel(keep_ref, arrived_ref, sum_ref, *, variables):
    for i in range(sum_ref.shape[0]):
        sum_ref[i] = joined(keep_ref[i], arrived_ref[i], variables).astype(BF16)


def swapped(array, axis, bit):
    count = lax.axis_size(axis)
    return lax.ppermute(array, axis, [(i, i ^ bit) for i in range(count)])


def from_members(array, members):
    others = {away: swapped(array, "member", away) for away in reversed(range(1, members))}
    return [array] + [others[away] for away in range(1, members)]


class Halving:
    def __init__(self, regions, members, rows):
        self.left = [("region", 1 << b) for b in reversed(range(shift_of(regions)))]
        self.left += [("member", 1 << b) for b in reversed(range(shift_of(members)))]
        self.rows = rows

    def half(self, step, packed):
        place = self.left.index(step)
        half = (1 << place, (1 << (len(self.left) - 1 - place)) * self.rows, packed)
        return half, (half[0], 2) + half[1:]

    def run(self, send, keep, steps, variables):
        packed = send.shape[-1]
        for i, (axis, bit) in enumerate(steps):
            arrived = swapped(send, axis, bit)
            self.left.remove((axis, bit))
            if i + 1 == len(steps):
                return keep, arrived
            half, both = self.half(steps[i + 1], packed)
            send, keep = on_core(
                functools.partial(
                    combine_kernel, axis=steps[i + 1][0], bit=steps[i + 1][1], variables=variables
                ),
                [(half, BF16), (half, F32)],
                keep.reshape(both), arrived.reshape(both),
            )


def unpack_kernel(w_dec_ref, *refs):
    sum_refs = refs[:-4]
    qkv_ref, out_ref, dec_ref, loss_ref = refs[-4:]
    width = out_ref.shape[-1]
    variables = dec_ref.shape[-1]
    step = padded(variables)
    start = 3 * width
    place = lax.axis_index("member")
    for away, ref in enumerate(sum_refs):
        at = place ^ away
        qkv_ref[at] = ref[:, :start].astype(F32)
        out_ref[at] = nn(ref[:, start : start + variables], w_dec_ref[...])
        dec_ref[at] = ref[:, start + step : start + step + variables].astype(F32)
    start += 2 * step
    last = sum_refs[0][0:1, start : start + 2].astype(F32)
    loss_ref[...] = last[:, 0:1] + last[:, 1:2]


def own_feature_kernel(grad_query_ref, grad_key_ref, grad_value_ref, w_ref, grad_ref):
    nodes, width = grad_query_ref.shape
    total = nt(grad_query_ref[...], w_ref[:, :width])
    total += nt(grad_key_ref[:nodes, :], w_ref[:, width : 2 * width])
    grad_ref[...] = total + nt(grad_value_ref[:nodes, :], w_ref[:, 2 * width :])


def latent_grad_kernel(
    hidden_ref, gain_ref, own_ref, from_left_ref, from_right_ref, border_ref, node_ref, grad_ref, rows_ref
):
    nodes = hidden_ref.shape[0]
    rim = from_left_ref.shape[0]
    rows_ref[:rim] = from_left_ref[...]
    rows_ref[rim:] = from_right_ref[...]
    mask = ones_where(iota((nodes, 2 * rim), 0) == border_ref[...])
    grad_rows = own_ref[...] + nn(mask, rows_ref[...])
    scaled, inverse = norm_parts(hidden_ref[...])
    scaled_grad = grad_rows * gain_ref[...]
    back = inverse * (
        scaled_grad
        - jnp.mean(scaled_grad, axis=-1, keepdims=True)
        - scaled * jnp.mean(scaled_grad * scaled, axis=-1, keepdims=True)
    )
    grad_ref[...] = (node_ref[...] + back).astype(BF16)


def swap_rims(head, tail):
    count = lax.axis_size("region")
    from_left = lax.ppermute(tail, "region", [(i, (i + 1) % count) for i in range(count)])
    from_right = lax.ppermute(head, "region", [((i + 1) % count, i) for i in range(count)])
    return from_left, from_right


def layer(
    latent,
    node_gain,
    w_qkv,
    w_out,
    edge_bias,
    edge_source,
    boundary,
    node_count,
    decoder_projection_weight,
    dec_source,
    dec_weight,
    state,
    target,
    area,
    var_weight,
):
    hidden = latent[0]
    nodes, width = hidden.shape
    rim = boundary.shape[1] // 2
    table_rows = nodes + 2 * rim
    sources = edge_source.T
    edges = sources.shape[0]
    w_decoder = decoder_projection_weight.T
    count = node_count[None]
    columns = edge_bias.shape[1]
    variables, points = state.shape
    regions, members = lax.axis_size("region"), lax.axis_size("member")
    total_points = points * regions
    gain = node_gain[None]
    rim_rows = ((rim, width), BF16)
    rim_columns = ((variables, rim), BF16)
    features, head, tail = on_core(
        norm_kernel,
        [((nodes, width), BF16), rim_rows, rim_rows],
        hidden, gain, boundary,
        fetched=3,
        scratch=[
            pltpu.VMEM((nodes, width), BF16), pltpu.VMEM((1, width), F32), pltpu.VMEM((1, 2 * rim), jnp.int32),
        ],
        mib=4,
    )
    left, right = swap_rims(head, tail)
    queries, own_edges, mix, w_qkv = on_core(
        project_kernel,
        [
            ((nodes, width), BF16), ((edges, nodes, 2 * width), BF16), ((table_rows, points), BF16),
            ((width, 3 * width), BF16),
        ],
        w_qkv, dec_source, dec_weight, sources, features,
        fetched=4,
        scratch=[
            pltpu.VMEM(dec_source.shape, jnp.int32), pltpu.VMEM(dec_weight.shape, F32),
            pltpu.VMEM((edges, nodes), jnp.int32),
        ],
        mib=12,
    )
    edge_rows = ((edges, nodes, width), BF16)
    node_out, projected, head, tail, probs, attended, keys, values, shares = on_core(
        attend_kernel,
        [
            ((nodes, width), BF16), ((variables, nodes), BF16), rim_columns, rim_columns,
            ((nodes, columns), F32), ((nodes, width), BF16), edge_rows, edge_rows, edge_rows,
        ],
        w_out, edge_bias, w_decoder, count, hidden, left, right, queries, own_edges, w_qkv, sources, boundary,
        fetched=3,
        scratch=[
            pltpu.VMEM((2 * rim, 2 * width), BF16), pltpu.VMEM((width, width), BF16),
            pltpu.VMEM((nodes, columns), F32), pltpu.VMEM((variables, width), BF16),
        ],
        mib=16,
    )
    out_left, out_right = swap_rims(head, tail)
    core = [("member", 1)]
    across = [("member", 1 << b) for b in range(1, shift_of(members))]
    own_tables = from_members(projected, members)
    (rims,) = on_core(join_kernel, [((variables, 2 * rim), BF16)], out_left, out_right)
    rim_tables = from_members(rims, members)
    grad, head, tail, loss = on_core(
        functools.partial(score_kernel, points=total_points),
        [((variables, points), BF16), rim_columns, rim_columns, ((1, LANES), F32)],
        state, target, area[None], var_weight[None], mix, *own_tables, *rim_tables,
    )
    back_left, back_right = swap_rims(head, tail)
    grad_own, hot = on_core(
        own_rows_kernel,
        [((variables, nodes), F32), ((table_rows, edges * nodes), BF16)],
        mix, grad, sources,
    )
    rows = width // (regions * members)
    pieces = regions * members // 2

    def halves(packed):
        return [((pieces, rows, packed), BF16), ((pieces, rows, packed), F32)]

    def whole(packed):
        return pltpu.VMEM((pieces, 2, rows, packed), F32)

    grad_node, grad_mixed, grad_value, value_send, value_keep = on_core(
        value_back_kernel,
        [((nodes, width), F32), ((nodes, width), BF16), ((table_rows, width), BF16)]
        + halves(width + 2 * LANES),
        count, grad_own, back_left, back_right, boundary, node_out, w_decoder,
        attended, w_out, shares, hot, features, left, right, loss,
        scratch=[pltpu.VMEM((edges * nodes, width), BF16), whole(width + 2 * LANES)],
        mib=16,
    )
    grad_query, key_edges = on_core(
        score_back_kernel,
        [((nodes, width), BF16), ((edges * nodes, width), BF16)],
        grad_mixed, probs, values, queries, keys,
    )
    grad_key, head, tail = on_core(
        query_back_kernel,
        [((table_rows, width), BF16), rim_rows, rim_rows],
        key_edges, hot, grad_value, w_qkv,
    )
    rim_left, rim_right = swap_rims(head, tail)
    query_send, query_keep = on_core(
        query_weight_kernel,
        halves(2 * width),
        features, left, right, grad_query, grad_key,
        scratch=[whole(2 * width)],
    )
    (own_feature,) = on_core(own_feature_kernel, [((nodes, width), F32)], grad_query, grad_key, grad_value, w_qkv)
    (grad_latent,) = on_core(
        latent_grad_kernel,
        [((nodes, width), BF16)],
        hidden, gain, own_feature, rim_left, rim_right, boundary, grad_node,
        scratch=[pltpu.VMEM((2 * rim, width), BF16)],
    )

    around = [("region", 1 << b) for b in range(shift_of(regions))]
    around[:2] = around[1::-1]
    value_sum, query_sum, key_sum = (Halving(regions, members, rows) for _ in range(3))
    value_parts = value_sum.run(value_send, value_keep, core + across + around[:1], variables)
    for chain in (query_sum, key_sum):
        chain.left.remove(core[0])
    steps = (across[0], around[0])
    arrived = swapped(query_send, *core[0])
    parts, views = [], []
    for chain, step in zip((query_sum, key_sum), steps):
        half, _ = chain.half(step, width)
        _, both = chain.half(step, 2 * width)
        parts += [(half, BF16), (half, F32)]
        views += [query_keep.reshape(both), arrived.reshape(both)]
    parts = on_core(functools.partial(part_kernel, steps=steps), parts, *views)
    query_parts = query_sum.run(*parts[:2], across + around[:1], None)
    key_parts = key_sum.run(*parts[2:], around[:1] + across, None)
    packed = 3 * width + 2 * LANES
    half, _ = value_sum.half(around[1], packed)
    views = []
    for chain in (query_parts, key_parts, value_parts):
        _, both = value_sum.half(around[1], chain[0].shape[-1])
        views += [part.reshape(both) for part in chain]
    send, keep = on_core(
        functools.partial(merge_kernel, axis=around[1][0], bit=around[1][1], variables=variables),
        [(half, BF16), (half, F32)],
        *views,
    )
    keep, arrived = value_sum.run(send, keep, around[1:], variables)
    piece = (1, rows, packed)
    (total,) = on_core(
        functools.partial(total_kernel, variables=variables), [(piece, BF16)],
        keep.reshape(piece), arrived.reshape(piece),
    )
    sums = from_members(total.reshape(rows, packed), members)
    share_qkv, share_out, share_dec, loss = on_core(
        unpack_kernel,
        [
            ((members, rows, 3 * width), F32), ((members, rows, width), F32),
            ((members, rows, variables), F32), ((1, 1), F32),
        ],
        w_decoder, *sums,
    )
    held = members * rows
    return (
        loss.reshape(()),
        share_qkv.reshape(held, 3 * width),
        share_out.reshape(held, width),
        share_dec.reshape(held, variables),
        grad_latent[None],
    )


def solution(mesh):
    placed = (
        P("member", "region", None),
        P(),
        P(),
        P(),
        P("region", None),
        P("region", None),
        P("region", None),
        P("region"),
        P(),
        P(None, "region"),
        P(None, "region"),
        P(None, "region"),
        P(None, "region"),
        P("region"),
        P(),
    )
    return jax.shard_map(
        layer,
        mesh=mesh,
        in_specs=placed,
        out_specs=(
            P(),
            P("region", None),
            P("region", None),
            P("region", None),
            P("member", "region", None),
        ),
        check_vma=False,
    )
```

```python
import functools
import math

import jax
import jax.numpy as jnp
from jax import lax
from jax.experimental import pallas as pl
from jax.experimental.pallas import tpu as pltpu
from jax.sharding import PartitionSpec as P


ALPHA = 0.95
NORM_EPS = 1e-05
SMOOTH_SQ = 0.25
SMOOTH_ROOT = 0.5
F32 = jnp.float32
BF16 = jnp.bfloat16
LANES = 128


def nn(left, right):
    return lax.dot_general(left, right, (((1,), (0,)), ((), ())), preferred_element_type=F32)


def nt(left, right):
    return lax.dot_general(left, right, (((1,), (1,)), ((), ())), preferred_element_type=F32)


def tn(left, right):
    return lax.dot_general(left, right, (((0,), (0,)), ((), ())), preferred_element_type=F32)


def on_core(kernel, outs, *args, fetched=0, scratch=(), mib=8):
    return pl.pallas_call(
        kernel,
        out_shape=[jax.ShapeDtypeStruct(s, d) for s, d in outs],
        in_specs=[pl.BlockSpec(memory_space=pltpu.HBM)] * fetched
        + [pl.BlockSpec(memory_space=pltpu.VMEM)] * (len(args) - fetched),
        out_specs=[pl.BlockSpec(memory_space=pltpu.VMEM)] * len(outs),
        scratch_shapes=list(scratch) + [pltpu.SemaphoreType.DMA((fetched,))] * (fetched > 0),
        compiler_params=pltpu.CompilerParams(vmem_limit_bytes=mib * 1024 * 1024),
    )(*[pltpu.with_memory_space_constraint(a, pltpu.HBM) for a in args[:fetched]], *args[fetched:])


def iota(shape, dim):
    return lax.broadcasted_iota(jnp.int32, shape, dim)


def ones_where(mask):
    return jnp.where(mask, 1.0, 0.0).astype(BF16)


def shift_of(size):
    assert size & (size - 1) == 0
    return size.bit_length() - 1


def head_map(rows, cols, row_size, col_size):
    return ones_where(
        (iota((rows, cols), 0) >> shift_of(row_size)) == (iota((rows, cols), 1) >> shift_of(col_size))
    )


def group_reduce(values, size, op):
    lanes = values.shape[1]
    lane = iota(values.shape, 1)
    step = 1
    while step < size:
        partner = jnp.where(
            (lane & step) == 0,
            pltpu.roll(values, lanes - step, 1),
            pltpu.roll(values, step, 1),
        )
        values = op(values, partner)
        step *= 2
    return values


def norm_parts(hidden):
    values = hidden.astype(F32)
    center = values - jnp.mean(values, axis=-1, keepdims=True)
    inverse = lax.rsqrt(jnp.mean(center * center, axis=-1, keepdims=True) + NORM_EPS)
    return center * inverse, inverse


def bit_of(axis, bit):
    return (lax.axis_index(axis) >> shift_of(bit)) & 1


def border_map(border_ref, nodes):
    return ones_where(iota((nodes, border_ref.shape[1]), 0) == border_ref[...])


def fetch(pairs, sems):
    copies = [pltpu.make_async_copy(a, b, sems.at[i]) for i, (a, b) in enumerate(pairs)]
    for copy in copies:
        copy.start()
    return copies


def norm_kernel(
    hidden_hbm, gain_hbm, border_hbm, features_ref, head_ref, tail_ref, hidden_ref, gain_ref, border_ref, sems
):
    pairs = ((hidden_hbm, hidden_ref), (gain_hbm, gain_ref), (border_hbm, border_ref))
    for copy in fetch(pairs, sems):
        copy.wait()
    scaled, _ = norm_parts(hidden_ref[...])
    features = (scaled * gain_ref[...]).astype(BF16)
    features_ref[...] = features
    rows = tn(border_map(border_ref, features.shape[0]), features).astype(BF16)
    rim = head_ref.shape[0]
    head_ref[...] = rows[:rim]
    tail_ref[...] = rows[rim:]


def project_kernel(
    w_hbm, src_hbm, weight_hbm, edge_hbm, features_ref, q_ref, own_ref, mix_ref, w_ref,
    src_ref, weight_ref, edge_ref, sems,
):
    pairs = ((src_hbm, src_ref), (weight_hbm, weight_ref), (w_hbm, w_ref), (edge_hbm, edge_ref))
    copies = fetch(pairs, sems)
    width = features_ref.shape[1]
    rows = iota(mix_ref.shape, 0)
    copies[0].wait()
    copies[1].wait()
    total = jnp.zeros(mix_ref.shape, F32)
    for j in range(src_ref.shape[0]):
        total += jnp.where(rows == src_ref[j : j + 1, :], weight_ref[j : j + 1, :], 0.0)
    mix_ref[...] = total.astype(BF16)
    copies[2].wait()
    qkv = nn(features_ref[...], w_ref[...]).astype(BF16)
    q_ref[...] = qkv[:, :width]
    key_value = qkv[:, width:]
    copies[3].wait()
    nodes = features_ref.shape[0]
    sources = edge_ref[...].astype(F32).T
    slot = iota((nodes, nodes), 1).astype(F32)
    for e in range(own_ref.shape[0]):
        own_ref[e] = nn(ones_where(slot == sources[:, e : e + 1]), key_value).astype(BF16)


def attend_kernel(
    w_out_hbm, bias_hbm, dec_hbm, count_ref, hidden_ref, left_ref, right_ref, q_ref, own_ref, w_ref,
    src_ref, border_ref, out_ref, projected_ref, head_ref, tail_ref, probs_ref, attended_ref, keys_ref, values_ref, shares_ref, table_ref,
    w_out_ref, bias_ref, dec_ref, sems,
):
    copies = fetch(((bias_hbm, bias_ref), (w_out_hbm, w_out_ref), (dec_hbm, dec_ref)), sems)
    nodes, width = hidden_ref.shape
    rim = left_ref.shape[0]
    edges = src_ref.shape[0]
    columns = bias_ref.shape[1]
    sources = src_ref[...].astype(F32).T
    head_size = width // (columns // edges)
    w_kv = w_ref[:, width:]
    table_ref[:rim] = nn(left_ref[...], w_kv).astype(BF16)
    table_ref[rim:] = nn(right_ref[...], w_kv).astype(BF16)
    table = table_ref[...]
    queries = q_ref[...].astype(F32)
    squeeze = head_map(width, columns, head_size, edges)
    expand = head_map(columns, width, edges, head_size)
    lane = iota((nodes, columns), 1) & (edges - 1)
    slot = (iota((nodes, table.shape[0]), 1) + nodes).astype(F32)
    scores = jnp.zeros((nodes, columns), F32)
    for e in range(edges):
        rows = nn(ones_where(slot == sources[:, e : e + 1]), table) + own_ref[e].astype(F32)
        keys_ref[e] = rows[:, :width].astype(BF16)
        values_ref[e] = rows[:, width:].astype(BF16)
        part = nn((queries * rows[:, :width]).astype(BF16), squeeze)
        scores = jnp.where(lane == e, part, scores)
    copies[0].wait()
    scores = scores / math.sqrt(head_size) + bias_ref[...]
    shifted = jnp.exp(scores - group_reduce(scores, edges, jnp.maximum))
    probs = shifted / group_reduce(shifted, edges, jnp.add)
    probs_ref[...] = probs
    total = jnp.zeros((nodes, width), F32)
    for e in range(edges):
        share = nn(jnp.where(lane == e, probs, 0.0).astype(BF16), expand)
        shares_ref[e] = share.astype(BF16)
        total += share * values_ref[e].astype(F32)
    attended = total.astype(BF16)
    attended_ref[...] = attended
    copies[1].wait()
    update = hidden_ref[...].astype(F32) + nn(attended, w_out_ref[...])
    live = iota((nodes, width), 0) < count_ref[...]
    node_out = jnp.where(live, update, 0.0).astype(BF16)
    out_ref[...] = node_out
    copies[2].wait()
    projected = nt(dec_ref[...], node_out).astype(BF16)
    projected_ref[...] = projected
    columns = nn(projected, border_map(border_ref, nodes)).astype(BF16)
    head_ref[...] = columns[:, :rim]
    tail_ref[...] = columns[:, rim:]


def join_kernel(left_ref, right_ref, rims_ref):
    rim = left_ref.shape[1]
    rims_ref[:, :rim] = left_ref[...]
    rims_ref[:, rim:] = right_ref[...]


def smooth_root(values):
    return values * values + SMOOTH_SQ


def score_kernel(state_ref, target_ref, area_ref, var_ref, mix_ref, *refs, points):
    grad_ref, head_ref, tail_ref, loss_ref, stack_ref = refs[-5:]
    table_refs = refs[:-5]
    members = len(table_refs) // 2
    fair = 1.0 - (1.0 - ALPHA) / members
    pair = fair / (2.0 * members * (members - 1))
    variables, nodes = table_refs[0].shape
    step = stack_ref.shape[0] // members
    for n in range(members):
        stack_ref[n * step : n * step + variables, :nodes] = table_refs[n][...]
        stack_ref[n * step : n * step + variables, nodes:] = table_refs[members + n][...]
    changes = nn(stack_ref[...], mix_ref[...])

    def change(n):
        return changes[n * step : n * step + variables]

    own = change(0)
    spread = jnp.zeros_like(own)
    slope = jnp.zeros_like(own)
    for n in range(members):
        gap = own - (change(n) if n else own)
        square = smooth_root(gap)
        inverse = lax.rsqrt(square)
        spread += square * inverse - SMOOTH_ROOT
        slope += gap * inverse
    gap = state_ref[...] + own - target_ref[...]
    square = smooth_root(gap)
    inverse = lax.rsqrt(square)
    square_map = (variables, variables)
    diagonal = iota(square_map, 0) == iota(square_map, 1)
    var = jnp.sum(jnp.where(diagonal, var_ref[...], 0.0), axis=1, keepdims=True)
    weight = area_ref[...] * var / variables
    term = (square * inverse - SMOOTH_ROOT) / members - pair * spread
    loss_ref[...] = jnp.full(loss_ref.shape, jnp.sum(term * weight) / points, F32)
    grad = ((gap * inverse / members - 2.0 * pair * slope) * weight).astype(BF16)
    grad_ref[...] = grad
    rim = head_ref.shape[1]
    nodes = mix_ref.shape[0] - 2 * rim
    columns = nt(grad, mix_ref[nodes:, :]).astype(BF16)
    head_ref[...] = columns[:, :rim]
    tail_ref[...] = columns[:, rim:]


def own_rows_kernel(mix_ref, grad_ref, src_ref, own_ref, hot_ref):
    nodes = own_ref.shape[1]
    own_ref[...] = nt(grad_ref[...], mix_ref[:nodes, :])
    slot = iota((hot_ref.shape[0], nodes), 0)
    for e in range(src_ref.shape[0]):
        hot_ref[:, e * nodes : (e + 1) * nodes] = ones_where(slot == src_ref[e : e + 1, :])


def padded(variables):
    return -(-variables // 8) * 8


def split_halves(mine, source_ref, send_ref, keep_ref):
    for i in range(send_ref.shape[0]):
        send_ref[i] = source_ref[i, 1 - mine].astype(BF16)
        keep_ref[i] = source_ref[i, mine]


def put(full_ref, start, values):
    shape = full_ref.shape[:3]
    full_ref[:, :, :, start : start + values.shape[1]] = values.reshape(*shape, values.shape[1])


def value_back_kernel(
    count_ref, own_ref, from_left_ref, from_right_ref, border_ref, node_out_ref, w_dec_ref,
    attended_ref, w_out_ref, shares_ref, hot_ref, features_ref, left_ref, right_ref, loss_ref,
    grad_ref, mixed_ref, grad_value_ref, send_ref, keep_ref, edge_ref, full_ref,
):
    nodes, width = grad_ref.shape
    rim = left_ref.shape[0]
    edges = shares_ref.shape[0]
    returned = jnp.concatenate([from_left_ref[...], from_right_ref[...]], axis=1)
    columns_grad = own_ref[...] + nt(returned, border_map(border_ref, nodes))
    live = iota(columns_grad.shape, 1) < count_ref[...]
    columns_grad = jnp.where(live, columns_grad, 0.0).astype(BF16)
    total = tn(columns_grad, w_dec_ref[...])
    grad_ref[...] = total
    rounded = total.astype(BF16)
    mixed = nt(rounded, w_out_ref[...]).astype(BF16)
    mixed_ref[...] = mixed
    for e in range(edges):
        edge_ref[e * nodes : (e + 1) * nodes, :] = shares_ref[e] * mixed
    grad_value = nn(hot_ref[...], edge_ref[...]).astype(BF16)
    grad_value_ref[...] = grad_value
    features = features_ref[...]
    total = tn(features, grad_value[:nodes])
    total += tn(left_ref[...], grad_value[nodes : nodes + rim])
    total += tn(right_ref[...], grad_value[nodes + rim :])
    put(full_ref, 0, total)
    variables = columns_grad.shape[0]
    step = padded(variables)
    columns_grad = jnp.concatenate(
        [columns_grad.astype(F32), jnp.zeros((step - variables, nodes), F32)], axis=0
    ).astype(BF16)
    loss = jnp.broadcast_to(loss_ref[0:1, 0:1], (2 * LANES - 2 * step, width))
    high = loss.astype(BF16).astype(F32)
    row = iota(loss.shape, 0)
    loss = jnp.where(row == 0, high, jnp.where(row == 1, loss - high, 0.0))
    few = [nn(columns_grad, attended_ref[...]), nn(columns_grad, node_out_ref[...]), loss]
    put(full_ref, width, jnp.concatenate(few, axis=0).T)
    split_halves(bit_of("member", 1), full_ref, send_ref, keep_ref)


def score_back_kernel(mixed_ref, probs_ref, values_ref, q_ref, keys_ref, grad_query_ref, edge_ref):
    nodes, width = mixed_ref.shape
    edges = values_ref.shape[0]
    columns = probs_ref.shape[1]
    head_size = width // (columns // edges)
    inv_root = 1.0 / math.sqrt(head_size)
    squeeze = head_map(width, columns, head_size, edges)
    expand = head_map(columns, width, edges, head_size)
    lane = iota((nodes, columns), 1) & (edges - 1)
    mixed = mixed_ref[...]
    probs = probs_ref[...]
    grad_probs = jnp.zeros((nodes, columns), F32)
    for e in range(edges):
        part = nn(mixed * values_ref[e], squeeze)
        grad_probs = jnp.where(lane == e, part, grad_probs)
    grad_scores = probs * (grad_probs - group_reduce(probs * grad_probs, edges, jnp.add))
    query = q_ref[...]
    total = jnp.zeros((nodes, width), F32)
    for e in range(edges):
        share = nn(jnp.where(lane == e, grad_scores, 0.0).astype(BF16), expand)
        total += share * keys_ref[e].astype(F32)
        edge_ref[e * nodes : (e + 1) * nodes, :] = share.astype(BF16) * query
    grad_query_ref[...] = (total * inv_root).astype(BF16)


def query_back_kernel(
    edge_ref, hot_ref, grad_value_ref, w_ref, grad_key_ref, head_ref, tail_ref, *, inv_root
):
    width = edge_ref.shape[1]
    rim = head_ref.shape[0]
    nodes = hot_ref.shape[0] - 2 * rim
    grad_key = (nn(hot_ref[...], edge_ref[...]) * inv_root).astype(BF16)
    grad_key_ref[...] = grad_key
    rows = nt(grad_key[nodes:], w_ref[:, width : 2 * width])
    rows += nt(grad_value_ref[nodes:, :], w_ref[:, 2 * width :])
    rows = rows.astype(BF16)
    head_ref[...] = rows[:rim]
    tail_ref[...] = rows[rim:]


def query_weight_kernel(
    features_ref, left_ref, right_ref, grad_query_ref, grad_key_ref, send_ref, keep_ref, full_ref
):
    nodes, width = features_ref.shape
    rim = left_ref.shape[0]
    features = features_ref[...]
    put(full_ref, 0, tn(features, grad_query_ref[...]))
    total = tn(features, grad_key_ref[:nodes, :])
    total += tn(left_ref[...], grad_key_ref[nodes : nodes + rim, :])
    total += tn(right_ref[...], grad_key_ref[nodes + rim :, :])
    put(full_ref, width, total)
    split_halves(bit_of("member", 1), full_ref, send_ref, keep_ref)


def joined(keep, arrived, variables):
    total = keep + arrived.astype(F32)
    if variables is None:
        return total
    last = total[..., -LANES:]
    lane = iota(last.shape, last.ndim - 1)
    at = 2 * padded(variables) - LANES
    loss = last[..., at : at + 1] + last[..., at + 1 : at + 2]
    high = loss.astype(BF16).astype(F32)
    last = jnp.where(lane == at, high, last)
    last = jnp.where(lane == at + 1, loss - high, last)
    return jnp.concatenate([total[..., :-LANES], last], axis=-1)


def combine_kernel(keep_in_ref, arrived_ref, send_ref, keep_ref, *, axis, bit, variables):
    mine = bit_of(axis, bit)
    for i in range(send_ref.shape[0]):
        away = 1 - mine
        send_ref[i] = joined(keep_in_ref[i, away], arrived_ref[i, away], variables).astype(BF16)
        keep_ref[i] = joined(keep_in_ref[i, mine], arrived_ref[i, mine], variables)


def part_kernel(
    keep_a_ref, in_a_ref, keep_b_ref, in_b_ref,
    query_send_ref, query_keep_ref, key_send_ref, key_keep_ref, *, steps,
):
    width = query_send_ref.shape[-1]
    cases = (
        (steps[0], keep_a_ref, in_a_ref, query_send_ref, query_keep_ref, slice(0, width)),
        (steps[1], keep_b_ref, in_b_ref, key_send_ref, key_keep_ref, slice(width, 2 * width)),
    )
    for (axis, bit), keep_in_ref, in_ref, send_ref, keep_ref, columns in cases:
        mine = bit_of(axis, bit)
        for at, out_ref in ((1 - mine, send_ref), (mine, keep_ref)):
            for i in range(send_ref.shape[0]):
                total = joined(keep_in_ref[i, at, :, columns], in_ref[i, at, :, columns], None)
                out_ref[i] = total.astype(out_ref.dtype)


def merge_kernel(*refs, axis, bit, variables):
    send_ref, keep_ref = refs[-2:]
    chains = [refs[i : i + 2] for i in range(0, len(refs) - 2, 2)]
    mine = bit_of(axis, bit)
    for at, out_ref in ((1 - mine, send_ref), (mine, keep_ref)):
        for i in range(send_ref.shape[0]):
            start = 0
            for n, (keep_in_ref, in_ref) in enumerate(chains):
                total = joined(
                    keep_in_ref[i, at], in_ref[i, at], variables if n + 1 == len(chains) else None
                )
                out_ref[i, :, start : start + total.shape[-1]] = total.astype(out_ref.dtype)
                start += total.shape[-1]


def total_kernel(keep_ref, arrived_ref, sum_ref, *, variables):
    for i in range(sum_ref.shape[0]):
        sum_ref[i] = joined(keep_ref[i], arrived_ref[i], variables).astype(BF16)


def swapped(array, axis, bit):
    count = lax.axis_size(axis)
    return lax.ppermute(array, axis, [(i, i ^ bit) for i in range(count)])


def from_members(array, members):
    others = {away: swapped(array, "member", away) for away in reversed(range(1, members))}
    return [array] + [others[away] for away in range(1, members)]


class Halving:
    def __init__(self, regions, members, rows):
        self.left = [("region", 1 << b) for b in reversed(range(shift_of(regions)))]
        self.left += [("member", 1 << b) for b in reversed(range(shift_of(members)))]
        self.rows = rows

    def half(self, step, packed):
        place = self.left.index(step)
        half = (1 << place, (1 << (len(self.left) - 1 - place)) * self.rows, packed)
        return half, (half[0], 2) + half[1:]

    def run(self, send, keep, steps, variables):
        packed = send.shape[-1]
        for i, (axis, bit) in enumerate(steps):
            arrived = swapped(send, axis, bit)
            self.left.remove((axis, bit))
            if i + 1 == len(steps):
                return keep, arrived
            half, both = self.half(steps[i + 1], packed)
            send, keep = on_core(
                functools.partial(
                    combine_kernel, axis=steps[i + 1][0], bit=steps[i + 1][1], variables=variables
                ),
                [(half, BF16), (half, F32)],
                keep.reshape(both), arrived.reshape(both),
            )


def unpack_kernel(w_dec_ref, *refs):
    sum_refs = refs[:-4]
    qkv_ref, out_ref, dec_ref, loss_ref = refs[-4:]
    width = out_ref.shape[-1]
    variables = dec_ref.shape[-1]
    step = padded(variables)
    start = 3 * width
    place = lax.axis_index("member")
    for away, ref in enumerate(sum_refs):
        at = place ^ away
        qkv_ref[at] = ref[:, :start].astype(F32)
        out_ref[at] = nn(ref[:, start : start + variables], w_dec_ref[...])
        dec_ref[at] = ref[:, start + step : start + step + variables].astype(F32)
    start += 2 * step
    last = sum_refs[0][0:1, start : start + 2].astype(F32)
    loss_ref[...] = last[:, 0:1] + last[:, 1:2]


def own_feature_kernel(grad_query_ref, grad_key_ref, grad_value_ref, w_ref, grad_ref):
    nodes, width = grad_query_ref.shape
    total = nt(grad_query_ref[...], w_ref[:, :width])
    total += nt(grad_key_ref[:nodes, :], w_ref[:, width : 2 * width])
    grad_ref[...] = total + nt(grad_value_ref[:nodes, :], w_ref[:, 2 * width :])


def latent_grad_kernel(
    hidden_ref, gain_ref, own_ref, from_left_ref, from_right_ref, border_ref, node_ref, grad_ref, rows_ref
):
    nodes = hidden_ref.shape[0]
    rim = from_left_ref.shape[0]
    rows_ref[:rim] = from_left_ref[...]
    rows_ref[rim:] = from_right_ref[...]
    mask = ones_where(iota((nodes, 2 * rim), 0) == border_ref[...])
    grad_rows = own_ref[...] + nn(mask, rows_ref[...])
    scaled, inverse = norm_parts(hidden_ref[...])
    scaled_grad = grad_rows * gain_ref[...]
    back = inverse * (
        scaled_grad
        - jnp.mean(scaled_grad, axis=-1, keepdims=True)
        - scaled * jnp.mean(scaled_grad * scaled, axis=-1, keepdims=True)
    )
    grad_ref[...] = (node_ref[...] + back).astype(BF16)


def swap_rims(head, tail):
    count = lax.axis_size("region")
    from_left = lax.ppermute(tail, "region", [(i, (i + 1) % count) for i in range(count)])
    from_right = lax.ppermute(head, "region", [((i + 1) % count, i) for i in range(count)])
    return from_left, from_right


def layer(
    latent,
    node_gain,
    w_qkv,
    w_out,
    edge_bias,
    edge_source,
    boundary,
    node_count,
    decoder_projection_weight,
    dec_source,
    dec_weight,
    state,
    target,
    area,
    var_weight,
):
    hidden = latent[0]
    nodes, width = hidden.shape
    rim = boundary.shape[1] // 2
    table_rows = nodes + 2 * rim
    sources = edge_source.T
    edges = sources.shape[0]
    w_decoder = decoder_projection_weight.T
    count = node_count[None]
    columns = edge_bias.shape[1]
    variables, points = state.shape
    regions, members = lax.axis_size("region"), lax.axis_size("member")
    total_points = points * regions
    gain = node_gain[None]
    rim_rows = ((rim, width), BF16)
    rim_columns = ((variables, rim), BF16)
    features, head, tail = on_core(
        norm_kernel,
        [((nodes, width), BF16), rim_rows, rim_rows],
        hidden, gain, boundary,
        fetched=3,
        scratch=[
            pltpu.VMEM((nodes, width), BF16), pltpu.VMEM((1, width), F32), pltpu.VMEM((1, 2 * rim), jnp.int32),
        ],
        mib=4,
    )
    left, right = swap_rims(head, tail)
    queries, own_edges, mix, w_qkv = on_core(
        project_kernel,
        [
            ((nodes, width), BF16), ((edges, nodes, 2 * width), BF16), ((table_rows, points), BF16),
            ((width, 3 * width), BF16),
        ],
        w_qkv, dec_source, dec_weight, sources, features,
        fetched=4,
        scratch=[
            pltpu.VMEM(dec_source.shape, jnp.int32), pltpu.VMEM(dec_weight.shape, F32),
            pltpu.VMEM((edges, nodes), jnp.int32),
        ],
        mib=12,
    )
    edge_rows = ((edges, nodes, width), BF16)
    node_out, projected, head, tail, probs, attended, keys, values, shares = on_core(
        attend_kernel,
        [
            ((nodes, width), BF16), ((variables, nodes), BF16), rim_columns, rim_columns,
            ((nodes, columns), F32), ((nodes, width), BF16), edge_rows, edge_rows, edge_rows,
        ],
        w_out, edge_bias, w_decoder, count, hidden, left, right, queries, own_edges, w_qkv, sources, boundary,
        fetched=3,
        scratch=[
            pltpu.VMEM((2 * rim, 2 * width), BF16), pltpu.VMEM((width, width), BF16),
            pltpu.VMEM((nodes, columns), F32), pltpu.VMEM((variables, width), BF16),
        ],
        mib=16,
    )
    out_left, out_right = swap_rims(head, tail)
    core = [("member", 1)]
    across = [("member", 1 << b) for b in range(1, shift_of(members))]
    own_tables = from_members(projected, members)
    (rims,) = on_core(join_kernel, [((variables, 2 * rim), BF16)], out_left, out_right)
    rim_tables = from_members(rims, members)
    grad, head, tail, loss = on_core(
        functools.partial(score_kernel, points=total_points),
        [((variables, points), BF16), rim_columns, rim_columns, ((1, LANES), F32)],
        state, target, area[None], var_weight[None], mix, *own_tables, *rim_tables,
        scratch=[pltpu.VMEM((members * (-(-variables // 16) * 16), table_rows), BF16)],
    )
    back_left, back_right = swap_rims(head, tail)
    grad_own, hot = on_core(
        own_rows_kernel,
        [((variables, nodes), F32), ((table_rows, edges * nodes), BF16)],
        mix, grad, sources,
    )
    rows = width // (regions * members)
    pieces = regions * members // 2

    def halves(packed):
        return [((pieces, rows, packed), BF16), ((pieces, rows, packed), F32)]

    def whole(packed):
        return pltpu.VMEM((pieces, 2, rows, packed), F32)

    grad_node, grad_mixed, grad_value, value_send, value_keep = on_core(
        value_back_kernel,
        [((nodes, width), F32), ((nodes, width), BF16), ((table_rows, width), BF16)]
        + halves(width + 2 * LANES),
        count, grad_own, back_left, back_right, boundary, node_out, w_decoder,
        attended, w_out, shares, hot, features, left, right, loss,
        scratch=[pltpu.VMEM((edges * nodes, width), BF16), whole(width + 2 * LANES)],
        mib=16,
    )
    grad_query, key_edges = on_core(
        score_back_kernel,
        [((nodes, width), BF16), ((edges * nodes, width), BF16)],
        grad_mixed, probs, values, queries, keys,
    )
    grad_key, head, tail = on_core(
        functools.partial(query_back_kernel, inv_root=1.0 / math.sqrt(width // (columns // edges))),
        [((table_rows, width), BF16), rim_rows, rim_rows],
        key_edges, hot, grad_value, w_qkv,
    )
    rim_left, rim_right = swap_rims(head, tail)
    query_send, query_keep = on_core(
        query_weight_kernel,
        halves(2 * width),
        features, left, right, grad_query, grad_key,
        scratch=[whole(2 * width)],
    )
    (own_feature,) = on_core(own_feature_kernel, [((nodes, width), F32)], grad_query, grad_key, grad_value, w_qkv)
    (grad_latent,) = on_core(
        latent_grad_kernel,
        [((nodes, width), BF16)],
        hidden, gain, own_feature, rim_left, rim_right, boundary, grad_node,
        scratch=[pltpu.VMEM((2 * rim, width), BF16)],
    )

    around = [("region", 1 << b) for b in range(shift_of(regions))]
    around[:2] = around[1::-1]
    value_sum, query_sum, key_sum = (Halving(regions, members, rows) for _ in range(3))
    value_parts = value_sum.run(value_send, value_keep, core + across + around[:1], variables)
    for chain in (query_sum, key_sum):
        chain.left.remove(core[0])
    steps = (across[0], around[0])
    arrived = swapped(query_send, *core[0])
    parts, views = [], []
    for chain, step in zip((query_sum, key_sum), steps):
        half, _ = chain.half(step, width)
        _, both = chain.half(step, 2 * width)
        parts += [(half, BF16), (half, F32)]
        views += [query_keep.reshape(both), arrived.reshape(both)]
    parts = on_core(functools.partial(part_kernel, steps=steps), parts, *views)
    query_parts = query_sum.run(*parts[:2], across + around[:1], None)
    key_parts = key_sum.run(*parts[2:], around[:1] + across, None)
    packed = 3 * width + 2 * LANES
    half, _ = value_sum.half(around[1], packed)
    views = []
    for chain in (query_parts, key_parts, value_parts):
        _, both = value_sum.half(around[1], chain[0].shape[-1])
        views += [part.reshape(both) for part in chain]
    send, keep = on_core(
        functools.partial(merge_kernel, axis=around[1][0], bit=around[1][1], variables=variables),
        [(half, BF16), (half, F32)],
        *views,
    )
    keep, arrived = value_sum.run(send, keep, around[1:], variables)
    piece = (1, rows, packed)
    (total,) = on_core(
        functools.partial(total_kernel, variables=variables), [(piece, BF16)],
        keep.reshape(piece), arrived.reshape(piece),
    )
    sums = from_members(total.reshape(rows, packed), members)
    share_qkv, share_out, share_dec, loss = on_core(
        unpack_kernel,
        [
            ((members, rows, 3 * width), F32), ((members, rows, width), F32),
            ((members, rows, variables), F32), ((1, 1), F32),
        ],
        w_decoder, *sums,
    )
    held = members * rows
    return (
        loss.reshape(()),
        share_qkv.reshape(held, 3 * width),
        share_out.reshape(held, width),
        share_dec.reshape(held, variables),
        grad_latent[None],
    )


def solution(mesh):
    placed = (
        P("member", "region", None),
        P(),
        P(),
        P(),
        P("region", None),
        P("region", None),
        P("region", None),
        P("region"),
        P(),
        P(None, "region"),
        P(None, "region"),
        P(None, "region"),
        P(None, "region"),
        P("region"),
        P(),
    )
    return jax.shard_map(
        layer,
        mesh=mesh,
        in_specs=placed,
        out_specs=(
            P(),
            P("region", None),
            P("region", None),
            P("region", None),
            P("member", "region", None),
        ),
        check_vma=False,
    )
```

```python
import functools
import math

import jax
import jax.numpy as jnp
from jax import lax
from jax.experimental import pallas as pl
from jax.experimental.pallas import tpu as pltpu
from jax.sharding import PartitionSpec as P


ALPHA = 0.95
NORM_EPS = 1e-05
SMOOTH_SQ = 0.25
SMOOTH_ROOT = 0.5
F32 = jnp.float32
BF16 = jnp.bfloat16
LANES = 128


def nn(left, right):
    return lax.dot_general(left, right, (((1,), (0,)), ((), ())), preferred_element_type=F32)


def nt(left, right):
    return lax.dot_general(left, right, (((1,), (1,)), ((), ())), preferred_element_type=F32)


def tn(left, right):
    return lax.dot_general(left, right, (((0,), (0,)), ((), ())), preferred_element_type=F32)


def on_core(kernel, outs, *args, fetched=0, scratch=(), mib=8):
    return pl.pallas_call(
        kernel,
        out_shape=[jax.ShapeDtypeStruct(s, d) for s, d in outs],
        in_specs=[pl.BlockSpec(memory_space=pltpu.HBM)] * fetched
        + [pl.BlockSpec(memory_space=pltpu.VMEM)] * (len(args) - fetched),
        out_specs=[pl.BlockSpec(memory_space=pltpu.VMEM)] * len(outs),
        scratch_shapes=list(scratch) + [pltpu.SemaphoreType.DMA((fetched,))] * (fetched > 0),
        compiler_params=pltpu.CompilerParams(vmem_limit_bytes=mib * 1024 * 1024),
    )(*[pltpu.with_memory_space_constraint(a, pltpu.HBM) for a in args[:fetched]], *args[fetched:])


def iota(shape, dim):
    return lax.broadcasted_iota(jnp.int32, shape, dim)


def ones_where(mask):
    return jnp.where(mask, 1.0, 0.0).astype(BF16)


def shift_of(size):
    assert size & (size - 1) == 0
    return size.bit_length() - 1


def head_map(rows, cols, row_size, col_size):
    return ones_where(
        (iota((rows, cols), 0) >> shift_of(row_size)) == (iota((rows, cols), 1) >> shift_of(col_size))
    )


def group_reduce(values, size, op):
    lanes = values.shape[1]
    lane = iota(values.shape, 1)
    step = 1
    while step < size:
        partner = jnp.where(
            (lane & step) == 0,
            pltpu.roll(values, lanes - step, 1),
            pltpu.roll(values, step, 1),
        )
        values = op(values, partner)
        step *= 2
    return values


def norm_parts(hidden):
    values = hidden.astype(F32)
    center = values - jnp.mean(values, axis=-1, keepdims=True)
    inverse = lax.rsqrt(jnp.mean(center * center, axis=-1, keepdims=True) + NORM_EPS)
    return center * inverse, inverse


def bit_of(axis, bit):
    return (lax.axis_index(axis) >> shift_of(bit)) & 1


def border_map(border_ref, nodes):
    return ones_where(iota((nodes, border_ref.shape[1]), 0) == border_ref[...])


def fetch(pairs, sems):
    copies = [pltpu.make_async_copy(a, b, sems.at[i]) for i, (a, b) in enumerate(pairs)]
    for copy in copies:
        copy.start()
    return copies


def norm_kernel(
    hidden_hbm, gain_hbm, border_hbm, features_ref, head_ref, tail_ref, hidden_ref, gain_ref, border_ref, sems
):
    pairs = ((hidden_hbm, hidden_ref), (gain_hbm, gain_ref), (border_hbm, border_ref))
    for copy in fetch(pairs, sems):
        copy.wait()
    scaled, _ = norm_parts(hidden_ref[...])
    features = (scaled * gain_ref[...]).astype(BF16)
    features_ref[...] = features
    rows = tn(border_map(border_ref, features.shape[0]), features).astype(BF16)
    rim = head_ref.shape[0]
    head_ref[...] = rows[:rim]
    tail_ref[...] = rows[rim:]


def project_kernel(
    w_hbm, src_hbm, weight_hbm, edge_hbm, features_ref, q_ref, own_ref, mix_ref, w_ref,
    src_ref, weight_ref, edge_ref, sems,
):
    pairs = ((src_hbm, src_ref), (weight_hbm, weight_ref), (w_hbm, w_ref), (edge_hbm, edge_ref))
    copies = fetch(pairs, sems)
    width = features_ref.shape[1]
    rows = iota(mix_ref.shape, 0)
    copies[0].wait()
    copies[1].wait()
    total = jnp.zeros(mix_ref.shape, F32)
    for j in range(src_ref.shape[0]):
        total += jnp.where(rows == src_ref[j : j + 1, :], weight_ref[j : j + 1, :], 0.0)
    mix_ref[...] = total.astype(BF16)
    copies[2].wait()
    qkv = nn(features_ref[...], w_ref[...]).astype(BF16)
    q_ref[...] = qkv[:, :width]
    key_value = qkv[:, width:]
    copies[3].wait()
    nodes = features_ref.shape[0]
    sources = edge_ref[...].astype(F32).T
    slot = iota((nodes, nodes), 1).astype(F32)
    for e in range(own_ref.shape[0]):
        own_ref[e] = nn(ones_where(slot == sources[:, e : e + 1]), key_value).astype(BF16)


def attend_kernel(
    w_out_hbm, bias_hbm, dec_hbm, count_ref, hidden_ref, left_ref, right_ref, q_ref, own_ref, w_ref,
    src_ref, border_ref, out_ref, projected_ref, head_ref, tail_ref, probs_ref, attended_ref, keys_ref, values_ref, shares_ref, table_ref,
    w_out_ref, bias_ref, dec_ref, sems,
):
    copies = fetch(((bias_hbm, bias_ref), (w_out_hbm, w_out_ref), (dec_hbm, dec_ref)), sems)
    nodes, width = hidden_ref.shape
    rim = left_ref.shape[0]
    edges = src_ref.shape[0]
    columns = bias_ref.shape[1]
    sources = src_ref[...].astype(F32).T
    head_size = width // (columns // edges)
    w_kv = w_ref[:, width:]
    table_ref[:rim] = nn(left_ref[...], w_kv).astype(BF16)
    table_ref[rim:] = nn(right_ref[...], w_kv).astype(BF16)
    table = table_ref[...]
    queries = q_ref[...].astype(F32)
    squeeze = head_map(width, columns, head_size, edges)
    expand = head_map(columns, width, edges, head_size)
    lane = iota((nodes, columns), 1) & (edges - 1)
    slot = (iota((nodes, table.shape[0]), 1) + nodes).astype(F32)
    scores = jnp.zeros((nodes, columns), F32)
    for e in range(edges):
        rows = nn(ones_where(slot == sources[:, e : e + 1]), table) + own_ref[e].astype(F32)
        keys_ref[e] = rows[:, :width].astype(BF16)
        values_ref[e] = rows[:, width:].astype(BF16)
        part = nn((queries * rows[:, :width]).astype(BF16), squeeze)
        scores = jnp.where(lane == e, part, scores)
    copies[0].wait()
    scores = scores / math.sqrt(head_size) + bias_ref[...]
    shifted = jnp.exp(scores - group_reduce(scores, edges, jnp.maximum))
    probs = shifted / group_reduce(shifted, edges, jnp.add)
    probs_ref[...] = probs
    total = jnp.zeros((nodes, width), F32)
    for e in range(edges):
        share = nn(jnp.where(lane == e, probs, 0.0).astype(BF16), expand)
        shares_ref[e] = share.astype(BF16)
        total += share * values_ref[e].astype(F32)
    attended = total.astype(BF16)
    attended_ref[...] = attended
    copies[1].wait()
    update = hidden_ref[...].astype(F32) + nn(attended, w_out_ref[...])
    live = iota((nodes, width), 0) < count_ref[...]
    node_out = jnp.where(live, update, 0.0).astype(BF16)
    out_ref[...] = node_out
    copies[2].wait()
    projected = nt(dec_ref[...], node_out).astype(BF16)
    projected_ref[...] = projected
    columns = nn(projected, border_map(border_ref, nodes)).astype(BF16)
    head_ref[...] = columns[:, :rim]
    tail_ref[...] = columns[:, rim:]


def join_kernel(left_ref, right_ref, rims_ref):
    rim = left_ref.shape[1]
    rims_ref[:, :rim] = left_ref[...]
    rims_ref[:, rim:] = right_ref[...]


def smooth_root(values):
    return values * values + SMOOTH_SQ


def score_kernel(state_ref, target_ref, area_ref, var_ref, mix_ref, *refs, points):
    grad_ref, head_ref, tail_ref, loss_ref, stack_ref = refs[-5:]
    table_refs = refs[:-5]
    members = len(table_refs) // 2
    fair = 1.0 - (1.0 - ALPHA) / members
    pair = fair / (2.0 * members * (members - 1))
    variables, nodes = table_refs[0].shape
    step = stack_ref.shape[0] // members
    for n in range(members):
        stack_ref[n * step : n * step + variables, :nodes] = table_refs[n][...]
        stack_ref[n * step : n * step + variables, nodes:] = table_refs[members + n][...]
    changes = nn(stack_ref[...], mix_ref[...])

    def change(n):
        return changes[n * step : n * step + variables]

    own = change(0)
    spread = jnp.zeros_like(own)
    slope = jnp.zeros_like(own)
    for n in range(members):
        gap = own - (change(n) if n else own)
        square = smooth_root(gap)
        inverse = lax.rsqrt(square)
        spread += square * inverse - SMOOTH_ROOT
        slope += gap * inverse
    gap = state_ref[...] + own - target_ref[...]
    square = smooth_root(gap)
    inverse = lax.rsqrt(square)
    square_map = (variables, variables)
    diagonal = iota(square_map, 0) == iota(square_map, 1)
    var = jnp.sum(jnp.where(diagonal, var_ref[...], 0.0), axis=1, keepdims=True)
    weight = area_ref[...] * var / variables
    term = (square * inverse - SMOOTH_ROOT) / members - pair * spread
    loss_ref[...] = jnp.full(loss_ref.shape, jnp.sum(term * weight) / points, F32)
    grad = ((gap * inverse / members - 2.0 * pair * slope) * weight).astype(BF16)
    grad_ref[...] = grad
    rim = head_ref.shape[1]
    nodes = mix_ref.shape[0] - 2 * rim
    columns = nt(grad, mix_ref[nodes:, :]).astype(BF16)
    head_ref[...] = columns[:, :rim]
    tail_ref[...] = columns[:, rim:]


def own_rows_kernel(mix_ref, grad_ref, src_ref, own_ref, hot_ref):
    nodes = own_ref.shape[1]
    own_ref[...] = nt(grad_ref[...], mix_ref[:nodes, :])
    slot = iota((hot_ref.shape[0], nodes), 0)
    for e in range(src_ref.shape[0]):
        hot_ref[:, e * nodes : (e + 1) * nodes] = ones_where(slot == src_ref[e : e + 1, :])


def padded(variables):
    return -(-variables // 8) * 8


def split_halves(mine, source_ref, send_ref, keep_ref):
    for i in range(send_ref.shape[0]):
        send_ref[i] = source_ref[i, 1 - mine].astype(BF16)
        keep_ref[i] = source_ref[i, mine]


def put(full_ref, start, values):
    shape = full_ref.shape[:3]
    full_ref[:, :, :, start : start + values.shape[1]] = values.reshape(*shape, values.shape[1])


def value_back_kernel(
    count_ref, own_ref, from_left_ref, from_right_ref, border_ref, node_out_ref, w_dec_ref,
    attended_ref, w_out_ref, shares_ref, hot_ref, features_ref, left_ref, right_ref, loss_ref,
    grad_ref, mixed_ref, grad_value_ref, send_ref, keep_ref, edge_ref, full_ref,
):
    nodes, width = grad_ref.shape
    rim = left_ref.shape[0]
    edges = shares_ref.shape[0]
    returned = jnp.concatenate([from_left_ref[...], from_right_ref[...]], axis=1)
    columns_grad = own_ref[...] + nt(returned, border_map(border_ref, nodes))
    live = iota(columns_grad.shape, 1) < count_ref[...]
    columns_grad = jnp.where(live, columns_grad, 0.0).astype(BF16)
    total = tn(columns_grad, w_dec_ref[...])
    grad_ref[...] = total
    rounded = total.astype(BF16)
    mixed = nt(rounded, w_out_ref[...]).astype(BF16)
    mixed_ref[...] = mixed
    for e in range(edges):
        edge_ref[e * nodes : (e + 1) * nodes, :] = shares_ref[e] * mixed
    grad_value = nn(hot_ref[...], edge_ref[...]).astype(BF16)
    grad_value_ref[...] = grad_value
    features = features_ref[...]
    total = tn(features, grad_value[:nodes])
    total += tn(left_ref[...], grad_value[nodes : nodes + rim])
    total += tn(right_ref[...], grad_value[nodes + rim :])
    put(full_ref, 0, total)
    variables = columns_grad.shape[0]
    step = padded(variables)
    columns_grad = jnp.concatenate(
        [columns_grad.astype(F32), jnp.zeros((step - variables, nodes), F32)], axis=0
    ).astype(BF16)
    loss = jnp.broadcast_to(loss_ref[0:1, 0:1], (2 * LANES - 2 * step, width))
    high = loss.astype(BF16).astype(F32)
    row = iota(loss.shape, 0)
    loss = jnp.where(row == 0, high, jnp.where(row == 1, loss - high, 0.0))
    few = [nn(columns_grad, attended_ref[...]), nn(columns_grad, node_out_ref[...]), loss]
    put(full_ref, width, jnp.concatenate(few, axis=0).T)
    split_halves(bit_of("member", 1), full_ref, send_ref, keep_ref)


def score_back_kernel(mixed_ref, probs_ref, values_ref, q_ref, keys_ref, grad_query_ref, edge_ref):
    nodes, width = mixed_ref.shape
    edges = values_ref.shape[0]
    columns = probs_ref.shape[1]
    head_size = width // (columns // edges)
    inv_root = 1.0 / math.sqrt(head_size)
    squeeze = head_map(width, columns, head_size, edges)
    expand = head_map(columns, width, edges, head_size)
    lane = iota((nodes, columns), 1) & (edges - 1)
    mixed = mixed_ref[...]
    probs = probs_ref[...]
    grad_probs = jnp.zeros((nodes, columns), F32)
    for e in range(edges):
        part = nn(mixed * values_ref[e], squeeze)
        grad_probs = jnp.where(lane == e, part, grad_probs)
    grad_scores = probs * (grad_probs - group_reduce(probs * grad_probs, edges, jnp.add))
    query = q_ref[...]
    total = jnp.zeros((nodes, width), F32)
    for e in range(edges):
        share = nn(jnp.where(lane == e, grad_scores, 0.0).astype(BF16), expand)
        total += share * keys_ref[e].astype(F32)
        edge_ref[e * nodes : (e + 1) * nodes, :] = share.astype(BF16) * query
    grad_query_ref[...] = (total * inv_root).astype(BF16)


def query_back_kernel(
    edge_ref, hot_ref, grad_value_ref, w_ref, grad_key_ref, head_ref, tail_ref, *, inv_root
):
    width = edge_ref.shape[1]
    rim = head_ref.shape[0]
    nodes = hot_ref.shape[0] - 2 * rim
    grad_key = (nn(hot_ref[...], edge_ref[...]) * inv_root).astype(BF16)
    grad_key_ref[...] = grad_key
    rows = nt(grad_key[nodes:], w_ref[:, width : 2 * width])
    rows += nt(grad_value_ref[nodes:, :], w_ref[:, 2 * width :])
    rows = rows.astype(BF16)
    head_ref[...] = rows[:rim]
    tail_ref[...] = rows[rim:]


def query_weight_kernel(
    features_ref, left_ref, right_ref, grad_query_ref, grad_key_ref, send_ref, keep_ref, full_ref
):
    nodes, width = features_ref.shape
    rim = left_ref.shape[0]
    features = features_ref[...]
    put(full_ref, 0, tn(features, grad_query_ref[...]))
    total = tn(features, grad_key_ref[:nodes, :])
    total += tn(left_ref[...], grad_key_ref[nodes : nodes + rim, :])
    total += tn(right_ref[...], grad_key_ref[nodes + rim :, :])
    put(full_ref, width, total)
    split_halves(bit_of("member", 1), full_ref, send_ref, keep_ref)


def joined(keep, arrived, variables):
    total = keep + arrived.astype(F32)
    if variables is None:
        return total
    last = total[..., -LANES:]
    lane = iota(last.shape, last.ndim - 1)
    at = 2 * padded(variables) - LANES
    loss = last[..., at : at + 1] + last[..., at + 1 : at + 2]
    high = loss.astype(BF16).astype(F32)
    last = jnp.where(lane == at, high, last)
    last = jnp.where(lane == at + 1, loss - high, last)
    return jnp.concatenate([total[..., :-LANES], last], axis=-1)


def combine_kernel(keep_in_ref, arrived_ref, send_ref, keep_ref, *, axis, bit, variables):
    mine = bit_of(axis, bit)
    for i in range(send_ref.shape[0]):
        away = 1 - mine
        send_ref[i] = joined(keep_in_ref[i, away], arrived_ref[i, away], variables).astype(BF16)
        keep_ref[i] = joined(keep_in_ref[i, mine], arrived_ref[i, mine], variables)


def part_kernel(
    keep_a_ref, in_a_ref, keep_b_ref, in_b_ref,
    query_send_ref, query_keep_ref, key_send_ref, key_keep_ref, *, steps,
):
    width = query_send_ref.shape[-1]
    cases = (
        (steps[0], keep_a_ref, in_a_ref, query_send_ref, query_keep_ref, slice(0, width)),
        (steps[1], keep_b_ref, in_b_ref, key_send_ref, key_keep_ref, slice(width, 2 * width)),
    )
    for (axis, bit), keep_in_ref, in_ref, send_ref, keep_ref, columns in cases:
        mine = bit_of(axis, bit)
        for at, out_ref in ((1 - mine, send_ref), (mine, keep_ref)):
            for i in range(send_ref.shape[0]):
                total = joined(keep_in_ref[i, at, :, columns], in_ref[i, at, :, columns], None)
                out_ref[i] = total.astype(out_ref.dtype)


def merge_kernel(*refs, axis, bit, variables):
    send_ref, keep_ref = refs[-2:]
    chains = [refs[i : i + 2] for i in range(0, len(refs) - 2, 2)]
    mine = bit_of(axis, bit)
    for at, out_ref in ((1 - mine, send_ref), (mine, keep_ref)):
        for i in range(send_ref.shape[0]):
            start = 0
            for n, (keep_in_ref, in_ref) in enumerate(chains):
                total = joined(
                    keep_in_ref[i, at], in_ref[i, at], variables if n + 1 == len(chains) else None
                )
                out_ref[i, :, start : start + total.shape[-1]] = total.astype(out_ref.dtype)
                start += total.shape[-1]


def total_kernel(keep_ref, arrived_ref, sum_ref, *, variables):
    for i in range(sum_ref.shape[0]):
        sum_ref[i] = joined(keep_ref[i], arrived_ref[i], variables).astype(BF16)


def swapped(array, axis, bit):
    count = lax.axis_size(axis)
    return lax.ppermute(array, axis, [(i, i ^ bit) for i in range(count)])


def from_members(array, members):
    others = {away: swapped(array, "member", away) for away in reversed(range(1, members))}
    return [array] + [others[away] for away in range(1, members)]


class Halving:
    def __init__(self, regions, members, rows):
        self.left = [("region", 1 << b) for b in reversed(range(shift_of(regions)))]
        self.left += [("member", 1 << b) for b in reversed(range(shift_of(members)))]
        self.rows = rows

    def half(self, step, packed):
        place = self.left.index(step)
        half = (1 << place, (1 << (len(self.left) - 1 - place)) * self.rows, packed)
        return half, (half[0], 2) + half[1:]

    def run(self, send, keep, steps, variables):
        packed = send.shape[-1]
        for i, (axis, bit) in enumerate(steps):
            arrived = swapped(send, axis, bit)
            self.left.remove((axis, bit))
            if i + 1 == len(steps):
                return keep, arrived
            half, both = self.half(steps[i + 1], packed)
            send, keep = on_core(
                functools.partial(
                    combine_kernel, axis=steps[i + 1][0], bit=steps[i + 1][1], variables=variables
                ),
                [(half, BF16), (half, F32)],
                keep.reshape(both), arrived.reshape(both),
            )


def unpack_kernel(w_dec_ref, *refs):
    sum_refs = refs[:-5]
    qkv_ref, out_ref, dec_ref, loss_ref, stack_ref = refs[-5:]
    width = out_ref.shape[-1]
    variables = dec_ref.shape[-1]
    step = padded(variables)
    start = 3 * width
    place = lax.axis_index("member")
    for away, ref in enumerate(sum_refs):
        at = place ^ away
        qkv_ref[at] = ref[:, :start].astype(F32)
        stack_ref[at] = ref[:, start : start + variables]
        dec_ref[at] = ref[:, start + step : start + step + variables].astype(F32)
    members, rows, _ = out_ref.shape
    if rows % 16 == 0:
        stacked = stack_ref[...].reshape(members * rows, variables)
        out_ref[...] = nn(stacked, w_dec_ref[...]).reshape(out_ref.shape)
    else:
        for n in range(members):
            out_ref[n] = nn(stack_ref[n], w_dec_ref[...])
    start += 2 * step
    last = sum_refs[0][0:1, start : start + 2].astype(F32)
    loss_ref[...] = last[:, 0:1] + last[:, 1:2]


def own_feature_kernel(grad_query_ref, grad_key_ref, grad_value_ref, w_ref, grad_ref):
    nodes, width = grad_query_ref.shape
    total = nt(grad_query_ref[...], w_ref[:, :width])
    total += nt(grad_key_ref[:nodes, :], w_ref[:, width : 2 * width])
    grad_ref[...] = total + nt(grad_value_ref[:nodes, :], w_ref[:, 2 * width :])


def latent_grad_kernel(
    hidden_ref, gain_ref, own_ref, from_left_ref, from_right_ref, border_ref, node_ref, grad_ref, rows_ref
):
    nodes = hidden_ref.shape[0]
    rim = from_left_ref.shape[0]
    rows_ref[:rim] = from_left_ref[...]
    rows_ref[rim:] = from_right_ref[...]
    mask = ones_where(iota((nodes, 2 * rim), 0) == border_ref[...])
    grad_rows = own_ref[...] + nn(mask, rows_ref[...])
    scaled, inverse = norm_parts(hidden_ref[...])
    scaled_grad = grad_rows * gain_ref[...]
    back = inverse * (
        scaled_grad
        - jnp.mean(scaled_grad, axis=-1, keepdims=True)
        - scaled * jnp.mean(scaled_grad * scaled, axis=-1, keepdims=True)
    )
    grad_ref[...] = (node_ref[...] + back).astype(BF16)


def swap_rims(head, tail):
    count = lax.axis_size("region")
    from_left = lax.ppermute(tail, "region", [(i, (i + 1) % count) for i in range(count)])
    from_right = lax.ppermute(head, "region", [((i + 1) % count, i) for i in range(count)])
    return from_left, from_right


def layer(
    latent,
    node_gain,
    w_qkv,
    w_out,
    edge_bias,
    edge_source,
    boundary,
    node_count,
    decoder_projection_weight,
    dec_source,
    dec_weight,
    state,
    target,
    area,
    var_weight,
):
    hidden = latent[0]
    nodes, width = hidden.shape
    rim = boundary.shape[1] // 2
    table_rows = nodes + 2 * rim
    sources = edge_source.T
    edges = sources.shape[0]
    w_decoder = decoder_projection_weight.T
    count = node_count[None]
    columns = edge_bias.shape[1]
    variables, points = state.shape
    regions, members = lax.axis_size("region"), lax.axis_size("member")
    total_points = points * regions
    gain = node_gain[None]
    rim_rows = ((rim, width), BF16)
    rim_columns = ((variables, rim), BF16)
    features, head, tail = on_core(
        norm_kernel,
        [((nodes, width), BF16), rim_rows, rim_rows],
        hidden, gain, boundary,
        fetched=3,
        scratch=[
            pltpu.VMEM((nodes, width), BF16), pltpu.VMEM((1, width), F32), pltpu.VMEM((1, 2 * rim), jnp.int32),
        ],
        mib=4,
    )
    left, right = swap_rims(head, tail)
    queries, own_edges, mix, w_qkv = on_core(
        project_kernel,
        [
            ((nodes, width), BF16), ((edges, nodes, 2 * width), BF16), ((table_rows, points), BF16),
            ((width, 3 * width), BF16),
        ],
        w_qkv, dec_source, dec_weight, sources, features,
        fetched=4,
        scratch=[
            pltpu.VMEM(dec_source.shape, jnp.int32), pltpu.VMEM(dec_weight.shape, F32),
            pltpu.VMEM((edges, nodes), jnp.int32),
        ],
        mib=12,
    )
    edge_rows = ((edges, nodes, width), BF16)
    node_out, projected, head, tail, probs, attended, keys, values, shares = on_core(
        attend_kernel,
        [
            ((nodes, width), BF16), ((variables, nodes), BF16), rim_columns, rim_columns,
            ((nodes, columns), F32), ((nodes, width), BF16), edge_rows, edge_rows, edge_rows,
        ],
        w_out, edge_bias, w_decoder, count, hidden, left, right, queries, own_edges, w_qkv, sources, boundary,
        fetched=3,
        scratch=[
            pltpu.VMEM((2 * rim, 2 * width), BF16), pltpu.VMEM((width, width), BF16),
            pltpu.VMEM((nodes, columns), F32), pltpu.VMEM((variables, width), BF16),
        ],
        mib=16,
    )
    out_left, out_right = swap_rims(head, tail)
    core = [("member", 1)]
    across = [("member", 1 << b) for b in range(1, shift_of(members))]
    own_tables = from_members(projected, members)
    (rims,) = on_core(join_kernel, [((variables, 2 * rim), BF16)], out_left, out_right)
    rim_tables = from_members(rims, members)
    grad, head, tail, loss = on_core(
        functools.partial(score_kernel, points=total_points),
        [((variables, points), BF16), rim_columns, rim_columns, ((1, LANES), F32)],
        state, target, area[None], var_weight[None], mix, *own_tables, *rim_tables,
        scratch=[pltpu.VMEM((members * (-(-variables // 16) * 16), table_rows), BF16)],
    )
    back_left, back_right = swap_rims(head, tail)
    grad_own, hot = on_core(
        own_rows_kernel,
        [((variables, nodes), F32), ((table_rows, edges * nodes), BF16)],
        mix, grad, sources,
    )
    rows = width // (regions * members)
    pieces = regions * members // 2

    def halves(packed):
        return [((pieces, rows, packed), BF16), ((pieces, rows, packed), F32)]

    def whole(packed):
        return pltpu.VMEM((pieces, 2, rows, packed), F32)

    grad_node, grad_mixed, grad_value, value_send, value_keep = on_core(
        value_back_kernel,
        [((nodes, width), F32), ((nodes, width), BF16), ((table_rows, width), BF16)]
        + halves(width + 2 * LANES),
        count, grad_own, back_left, back_right, boundary, node_out, w_decoder,
        attended, w_out, shares, hot, features, left, right, loss,
        scratch=[pltpu.VMEM((edges * nodes, width), BF16), whole(width + 2 * LANES)],
        mib=16,
    )
    grad_query, key_edges = on_core(
        score_back_kernel,
        [((nodes, width), BF16), ((edges * nodes, width), BF16)],
        grad_mixed, probs, values, queries, keys,
    )
    grad_key, head, tail = on_core(
        functools.partial(query_back_kernel, inv_root=1.0 / math.sqrt(width // (columns // edges))),
        [((table_rows, width), BF16), rim_rows, rim_rows],
        key_edges, hot, grad_value, w_qkv,
    )
    rim_left, rim_right = swap_rims(head, tail)
    query_send, query_keep = on_core(
        query_weight_kernel,
        halves(2 * width),
        features, left, right, grad_query, grad_key,
        scratch=[whole(2 * width)],
    )
    (own_feature,) = on_core(own_feature_kernel, [((nodes, width), F32)], grad_query, grad_key, grad_value, w_qkv)
    (grad_latent,) = on_core(
        latent_grad_kernel,
        [((nodes, width), BF16)],
        hidden, gain, own_feature, rim_left, rim_right, boundary, grad_node,
        scratch=[pltpu.VMEM((2 * rim, width), BF16)],
    )

    around = [("region", 1 << b) for b in range(shift_of(regions))]
    around[:2] = around[1::-1]
    value_sum, query_sum, key_sum = (Halving(regions, members, rows) for _ in range(3))
    value_parts = value_sum.run(value_send, value_keep, core + across + around[:1], variables)
    for chain in (query_sum, key_sum):
        chain.left.remove(core[0])
    steps = (across[0], around[0])
    arrived = swapped(query_send, *core[0])
    parts, views = [], []
    for chain, step in zip((query_sum, key_sum), steps):
        half, _ = chain.half(step, width)
        _, both = chain.half(step, 2 * width)
        parts += [(half, BF16), (half, F32)]
        views += [query_keep.reshape(both), arrived.reshape(both)]
    parts = on_core(functools.partial(part_kernel, steps=steps), parts, *views)
    query_parts = query_sum.run(*parts[:2], across + around[:1], None)
    key_parts = key_sum.run(*parts[2:], around[:1] + across, None)
    packed = 3 * width + 2 * LANES
    half, _ = value_sum.half(around[1], packed)
    views = []
    for chain in (query_parts, key_parts, value_parts):
        _, both = value_sum.half(around[1], chain[0].shape[-1])
        views += [part.reshape(both) for part in chain]
    send, keep = on_core(
        functools.partial(merge_kernel, axis=around[1][0], bit=around[1][1], variables=variables),
        [(half, BF16), (half, F32)],
        *views,
    )
    keep, arrived = value_sum.run(send, keep, around[1:], variables)
    piece = (1, rows, packed)
    (total,) = on_core(
        functools.partial(total_kernel, variables=variables), [(piece, BF16)],
        keep.reshape(piece), arrived.reshape(piece),
    )
    sums = from_members(total.reshape(rows, packed), members)
    share_qkv, share_out, share_dec, loss = on_core(
        unpack_kernel,
        [
            ((members, rows, 3 * width), F32), ((members, rows, width), F32),
            ((members, rows, variables), F32), ((1, 1), F32),
        ],
        w_decoder, *sums,
        scratch=[pltpu.VMEM((members, rows, variables), BF16)],
    )
    held = members * rows
    return (
        loss.reshape(()),
        share_qkv.reshape(held, 3 * width),
        share_out.reshape(held, width),
        share_dec.reshape(held, variables),
        grad_latent[None],
    )


def solution(mesh):
    placed = (
        P("member", "region", None),
        P(),
        P(),
        P(),
        P("region", None),
        P("region", None),
        P("region", None),
        P("region"),
        P(),
        P(None, "region"),
        P(None, "region"),
        P(None, "region"),
        P(None, "region"),
        P("region"),
        P(),
    )
    return jax.shard_map(
        layer,
        mesh=mesh,
        in_specs=placed,
        out_specs=(
            P(),
            P("region", None),
            P("region", None),
            P("region", None),
            P("member", "region", None),
        ),
        check_vma=False,
    )
```
